32 devices in a mesh: region: 4 (over z), dom: 8 (over y, x, core).
Axes of the slice: x: 2, y: 2, z: 4, core: 2. Of those that a mesh axis runs over, the one named last changes fastest.
Arguments:
- fine_blocks: bfloat16 [1536, 7, 128, 128], P(('region', 'dom')), may hold values from -6 to 6
- interp: bfloat16 [1536, 8192], P(('region', 'dom')), may hold values from -0.5 to 0.5
- fine_cols: int32 [1536, 7], P(('region', 'dom')), may hold values from 0 to 1535, as said below
- fine_slot: int32 [1536, 7], P(('region', 'dom')), may hold values from 0 to 6
- fine_owner: int32 [1536, 1], P(('region', 'dom')), may hold values from 0 to 7; in each aligned block of 48 rows (0 to 47, 48 to 95, ...) at most 6 rows name the same one
- fine_place: int32 [1536], P(('region', 'dom')), may hold values from 0 to 23
- coarse_interp: bfloat16 [768, 2048], P(('region', 'dom')), may hold values from -0.75 to 0.75
- coarse_cols: int32 [768, 7], P(('region', 'dom')), may hold values from 0 to 767, as said below
- coarse_slot: int32 [768, 7], P(('region', 'dom')), may hold values from 0 to 6
- coarse_owner: int32 [768, 1], P(('region', 'dom')), may hold values from 0 to 7; in each aligned block of 24 rows (0 to 23, 24 to 47, ...) at most 3 rows name the same one
- coarse_place: int32 [768], P(('region', 'dom')), may hold values from 0 to 11
Outputs:
- coarse_blocks: bfloat16 [768, 7, 4096], P(('region', 'dom'))
- coarse2_blocks: bfloat16 [384, 7, 1024], P(('region', 'dom'))
The draws below stay inside these ranges and needn't reach their ends.
Inputs may be any that keep to these rules, and one draw needn't show every extreme that they name: fine_cols[i, 0] = i; every other entry names a fine row held by the device of the same dom index in the same region or in an adjacent region. coarse_cols[q, 0] = q; every other entry names a coarse row of the same region or of an adjacent region. `fine_owner`: among the rows of one device, no owner is named more than 6 times, a bound that some block reaches. `coarse_owner`: among the rows of one device, no owner is named more than 3 times, a bound that some block reaches.
All inputs are finite; a program needn't handle non-finite values.
Results may differ from the reference program's by a relative error of at most 0.0065.
Values may be sent and summed in bfloat16 or wider, within the bound.
No kernel may reach another device: no remote copies, remote signals or barrier semaphores. Data moves between devices by JAX's collectives and lax.ppermute only.
A program may use at most 128 MiB of HBM per device.

```python
import math
import jax
import jax.numpy as jnp
import numpy as np
from jax import lax

BF = 128
BC = 64
BC2 = 32
STENCIL = 7
ROWS_DEV = 48
C_DEV = 24
C2_DEV = 12
CAP1 = 6
CAP2 = 3
FINE_ROWS = 1536
COARSE_ROWS = 768
N_REGION = 4
N_DOM = 8


def draw_fine_cols(key, part):
    total = ROWS_DEV * N_REGION * N_DOM
    rows = jnp.arange(total, dtype=jnp.int32)
    region = rows // (N_DOM * ROWS_DEV)
    within = rows % (N_DOM * ROWS_DEV) // ROWS_DEV
    first, second = jax.random.split(jax.random.fold_in(key, 11))
    moves = jax.random.randint(first, (total, STENCIL - 1), -1, 2)
    target = region[:, None] + moves
    target = jnp.where(target < 0, 1, target)
    target = jnp.where(target >= N_REGION, N_REGION - 2, target)
    local = jax.random.randint(second, (total, STENCIL - 1), 0, ROWS_DEV)
    others = (target * N_DOM + within[:, None]) * ROWS_DEV + local
    return jnp.concatenate([rows[:, None], others], axis=1).astype(jnp.int32)


def draw_coarse_cols(key, part):
    owned = ROWS_DEV // 2
    span = N_DOM * owned
    total = span * N_REGION
    rows = jnp.arange(total, dtype=jnp.int32)
    region = rows // span
    first, second = jax.random.split(jax.random.fold_in(key, 23))
    moves = jax.random.randint(first, (total, STENCIL - 1), -1, 2)
    target = region[:, None] + moves
    target = jnp.where(target < 0, 1, target)
    target = jnp.where(target >= N_REGION, N_REGION - 2, target)
    inside = jax.random.randint(second, (total, STENCIL - 1), 0, span)
    others = target * span + inside
    return jnp.concatenate([rows[:, None], others], axis=1).astype(jnp.int32)


def touch_ends(array, stream_key, low, top_value):
    longest = array.shape.index(max(array.shape))
    spots = []
    for shift in (0, 1):
        where = [jax.random.randint(jax.random.fold_in(stream_key, axis), (), 0, length) for axis, length in enumerate(array.shape)]
        where[longest] = (where[longest] + shift) % array.shape[longest]
        spots.append(tuple(where))
    return array.at[spots[0]].set(low).at[spots[1]].set(top_value)


def block_levels(key, extent, cuts, low, high):
    level = 1.0
    for dim, shards_of in cuts:
        steps = jax.random.uniform(jax.random.fold_in(jax.random.fold_in(key, 6), dim), (shards_of,), jnp.float32, low / len(cuts), high / len(cuts))
        level = level * jnp.repeat(jnp.exp(steps), extent[dim] // shards_of).reshape((-1,) + (1,) * (len(extent) - 1 - dim))
    return level


def shared_out(rng, own, number, rows, amount, top, bound, skew):
    order = jax.random.permutation(rng, amount)
    heavy_load, common = load_shares(amount, rows * top, bound, skew, True), load_shares(amount, rows * top, bound, skew, False)
    places = jnp.arange(amount)

    def named(sizes, offset_by):
        used = int((sizes > 0).sum())
        fixed = max(1, used // 4)
        moved = fixed + (places - fixed + offset_by * (used - fixed)) % max(1, amount - fixed)
        return jnp.zeros((amount,), jnp.int32).at[order[jnp.where(places < fixed, places, moved)]].set(jnp.asarray(sizes, jnp.int32))

    sizes = jnp.where(number % 4 == 0, named(heavy_load, number // 4), named(common, number - number // 4 - 1))
    mixed = jax.random.permutation(jax.random.fold_in(own, 3), amount)
    source_of, receiver = mixed[0:amount // 2 * 2:2], mixed[1:amount // 2 * 2:2]
    slack = jnp.minimum(sizes[source_of] - 1, bound - sizes[receiver]) // 2
    slack = jnp.where((source_of == order[0]) | (receiver == order[0]) | (sizes[receiver] == 0), 0, jnp.maximum(slack, 0))
    moved = jax.random.randint(jax.random.fold_in(own, 4), (amount // 2,), 0, 1 << 20) % (slack + 1)
    sizes = sizes.at[source_of].add(-moved).at[receiver].add(moved)
    members = jnp.searchsorted(jnp.cumsum(sizes), jnp.arange(rows * top), side="right").astype(jnp.int32)
    grid = members.reshape(top, rows).T
    grid = grid[jax.random.permutation(jax.random.fold_in(own, 1), rows)]
    offset_by = jax.random.randint(jax.random.fold_in(own, 2), (rows, 1), 0, top)
    return jnp.take_along_axis(grid, (jnp.arange(top)[None, :] + offset_by) % top, axis=1)


def load_shares(amount, total, limit, skew, full):
    portions = [(1 << 20) // math.isqrt(rank ** skew) + 1 for rank in range(1, amount + 1)]
    largest = limit if full else min(limit, max(-(-total // amount), total * portions[0] // sum(portions)))
    least = 1 if total - largest >= amount - 1 else 0
    holding, spare = [largest] + [least] * (amount - 1), total - largest - least * (amount - 1)
    while spare > 0:
        movable = [i for i in range(1, amount) if holding[i] < largest] or [i for i in range(1, amount) if holding[i] < limit]
        whole, remaining = sum([portions[i] for i in movable]), spare
        for i in movable:
            addition = min(limit - holding[i], max(1, remaining * portions[i] // whole), spare)
            holding[i] = holding[i] + addition
            spare = spare - addition
    return np.array(holding)


def bell_draw(own_key, shape, scale, reach, pieces=(), kind=jnp.bfloat16):
    values = scale * jax.random.normal(own_key, shape, jnp.float32)
    if pieces:
        values = values * block_levels(own_key, shape, pieces, -0.22, 0.18)
    return jnp.clip(values, -reach, reach).astype(kind)


def setup_inputs(seed: int = 0) -> dict:
    seeds = jax.random.split(jax.random.key(seed), 12)
    fine_blocks = bell_draw(seeds[0], (FINE_ROWS, STENCIL, BF, BF), 1.0, 6.0, ((0, 32),))
    interp = bell_draw(seeds[1], (FINE_ROWS, BF * BC), BF ** -0.5, 0.5, ((0, 32),))
    fine_cols = draw_fine_cols(jax.random.fold_in(seeds[11], 71), 0)
    fine_slot = touch_ends(jax.random.randint(seeds[3], (FINE_ROWS, STENCIL), 0, STENCIL), jax.random.fold_in(seeds[3], 1), 0, STENCIL - 1).astype(jnp.int32)
    fine_owner_keys = jax.random.split(jax.random.fold_in(seeds[4], 1), FINE_ROWS // ROWS_DEV)
    fine_owner_turns = jax.random.permutation(jax.random.fold_in(seeds[4], 3), FINE_ROWS // ROWS_DEV)
    fine_owner = jax.vmap(lambda own, number: shared_out(jax.random.fold_in(seeds[4], 2), own, number, ROWS_DEV, N_DOM, 1, CAP1, 2))(fine_owner_keys, fine_owner_turns).reshape((FINE_ROWS, 1))
    fine_place = touch_ends(jax.random.randint(seeds[5], (FINE_ROWS,), 0, C_DEV), jax.random.fold_in(seeds[5], 1), 0, C_DEV - 1).astype(jnp.int32)
    coarse_interp = bell_draw(seeds[6], (COARSE_ROWS, BC * BC2), BC ** -0.5, 0.75, ((0, 32),))
    coarse_cols = draw_coarse_cols(jax.random.fold_in(seeds[11], 71), 0)
    coarse_slot = touch_ends(jax.random.randint(seeds[8], (COARSE_ROWS, STENCIL), 0, STENCIL), jax.random.fold_in(seeds[8], 1), 0, STENCIL - 1).astype(jnp.int32)
    coarse_owner_keys = jax.random.split(jax.random.fold_in(seeds[9], 1), COARSE_ROWS // C_DEV)
    coarse_owner_turns = jax.random.permutation(jax.random.fold_in(seeds[9], 3), COARSE_ROWS // C_DEV)
    coarse_owner = jax.vmap(lambda own, number: shared_out(jax.random.fold_in(seeds[9], 2), own, number, C_DEV, N_DOM, 1, CAP2, 2))(coarse_owner_keys, coarse_owner_turns).reshape((COARSE_ROWS, 1))
    coarse_place = touch_ends(jax.random.randint(seeds[10], (COARSE_ROWS,), 0, C2_DEV), jax.random.fold_in(seeds[10], 1), 0, C2_DEV - 1).astype(jnp.int32)
    return dict(fine_blocks=fine_blocks, interp=interp, fine_cols=fine_cols, fine_slot=fine_slot, fine_owner=fine_owner, fine_place=fine_place, coarse_interp=coarse_interp, coarse_cols=coarse_cols, coarse_slot=coarse_slot, coarse_owner=coarse_owner, coarse_place=coarse_place)


def one_level(blocks, interp_rows, cols, slot, owner, place, width, narrow, per_dev, owned, devices):
    stencil = blocks.shape[1]
    count = blocks.shape[0]
    interp_all = interp_rows.reshape(count, width, narrow)
    owner_col = owner[:, 0]
    letters = jnp.arange(stencil, dtype=jnp.int32)

    def step(total, index):
        start = (index * per_dev).astype(jnp.int32)
        block_rows = lax.dynamic_slice_in_dim(blocks, start, per_dev, 0).astype(jnp.float32)
        col_rows = lax.dynamic_slice_in_dim(cols, start, per_dev, 0)
        picked = interp_all[col_rows].astype(jnp.float32)
        product = jnp.einsum('rkab,rkbc->rkac', block_rows, picked).astype(jnp.bfloat16)
        product = lax.optimization_barrier(product).astype(jnp.float32)
        own_rows = lax.dynamic_slice_in_dim(interp_all, start, per_dev, 0).astype(jnp.float32)
        term = jnp.einsum('rac,rkad->rkcd', own_rows, product).reshape(per_dev, stencil, narrow * narrow)
        slot_rows = lax.dynamic_slice_in_dim(slot, start, per_dev, 0)
        choose = (slot_rows[:, :, None] == letters[None, None, :]).astype(jnp.float32)
        slotted = jnp.einsum('rks,rkx->rsx', choose, term, precision=lax.Precision.HIGHEST)
        rows = start + jnp.arange(per_dev, dtype=jnp.int32)
        region = rows // (N_DOM * per_dev)
        owner_rows = lax.dynamic_slice_in_dim(owner_col, start, per_dev, 0)
        place_rows = lax.dynamic_slice_in_dim(place, start, per_dev, 0)
        target = ((region * N_DOM + owner_rows) * owned + place_rows).astype(jnp.int32)
        return total.at[target].add(slotted), None

    initial = jnp.zeros((devices * owned, stencil, narrow * narrow), jnp.float32)
    total, _ = lax.scan(step, initial, jnp.arange(devices, dtype=jnp.int32))
    return total.astype(jnp.bfloat16)


def reference(fine_blocks, interp, fine_cols, fine_slot, fine_owner, fine_place, coarse_interp, coarse_cols, coarse_slot, coarse_owner, coarse_place):
    devices = N_REGION * N_DOM
    coarse_blocks = one_level(fine_blocks, interp, fine_cols, fine_slot, fine_owner, fine_place, BF, BC, ROWS_DEV, C_DEV, devices)
    coarse_square = coarse_blocks.reshape(COARSE_ROWS, STENCIL, BC, BC)
    coarse2_blocks = one_level(coarse_square, coarse_interp, coarse_cols, coarse_slot, coarse_owner, coarse_place, BC, BC2, C_DEV, C2_DEV, devices)
    return (coarse_blocks, coarse2_blocks)
```

```python
import functools

import jax
import jax.numpy as jnp
from jax import lax
from jax.experimental import pallas as pl
from jax.experimental.pallas import tpu as pltpu
from jax.sharding import PartitionSpec as P

BF16 = jnp.bfloat16
F32 = jnp.float32
I32 = jnp.int32
LANES = 128
VMEM_LIMIT = 48 * 1024 * 1024


def vmem():
    return pl.BlockSpec(memory_space=pltpu.VMEM)


def smem():
    return pl.BlockSpec(memory_space=pltpu.SMEM)


def hbm():
    return pl.BlockSpec(memory_space=pl.ANY)


def params():
    return pltpu.CompilerParams(vmem_limit_bytes=VMEM_LIMIT)


def low_lanes(shape, bound):
    return lax.broadcasted_iota(I32, shape, len(shape) - 1) < bound


def exchange(cells, axis, offset):
    count = lax.axis_size(axis)
    return lax.ppermute(cells, axis, [(i, i ^ offset) for i in range(count)])


def neighbours(cells, axis):
    count = lax.axis_size(axis)
    previous = lax.ppermute(cells, axis, [(i, i + 1) for i in range(count - 1)])
    following = lax.ppermute(cells, axis, [(i + 1, i) for i in range(count - 1)])
    return previous, following


def halves_kernel(flat_ref, out_ref, wide_ref):
    rows = flat_ref.shape[0]
    deep = flat_ref.shape[1] // LANES
    half = deep // 2
    group = 16
    left = low_lanes((group, LANES), LANES // 2)
    for g in range(rows // group):
        for t in range(half):
            upper = flat_ref[pl.ds(g * group, group), pl.ds(t * LANES, LANES)].astype(F32)
            lower = flat_ref[pl.ds(g * group, group), pl.ds((t + half) * LANES, LANES)].astype(F32)
            even = jnp.where(left, upper, pltpu.roll(lower, LANES // 2, 1))
            odd = jnp.where(left, pltpu.roll(upper, LANES // 2, 1), lower)
            wide_ref[pl.ds(g * group * deep + 2 * t, group, stride=deep), :] = even
            wide_ref[pl.ds(g * group * deep + 2 * t + 1, group, stride=deep), :] = odd
    for r in range(rows):
        out_ref[r] = wide_ref[pl.ds(r * deep, deep), :].astype(BF16)


def halves(flat):
    rows, size = flat.shape
    deep = size // LANES
    return pl.pallas_call(
        halves_kernel,
        out_shape=jax.ShapeDtypeStruct((rows, deep, LANES), BF16),
        in_specs=[vmem()],
        out_specs=vmem(),
        scratch_shapes=[pltpu.VMEM((rows * deep, LANES), F32)],
        compiler_params=params(),
    )(flat)


def index_kernel(
    where_ref,
    cols_ref,
    slot_ref,
    owner_ref,
    place_ref,
    slot2_ref,
    owner2_ref,
    place2_ref,
    source_ref,
    near_ref,
    target_ref,
    source2_ref,
    count_ref,
    *,
    parts,
    capacity,
    capacity2,
    owned,
    owned2,
):
    region = where_ref[0]
    dom = where_ref[1]
    stencil, rows = cols_ref.shape
    rows2 = slot2_ref.shape[1]
    span = parts * rows
    first = region * span
    slots = parts * capacity
    slots2 = parts * capacity2

    def clear_counts(d, carry):
        count_ref[d] = 0
        return carry

    if slots > rows or slots2 > rows2:

        def clear(p, carry):
            source_ref[p] = 0
            for k in range(stencil):
                near_ref[p * stencil + k] = 0
                target_ref[p * stencil + k] = -1
            return carry

        lax.fori_loop(0, slots, clear, 0)

        def clear2(p, carry):
            source2_ref[p] = 0
            for k in range(stencil):
                target_ref[(slots + p) * stencil + k] = -1
            return carry

        lax.fori_loop(0, slots2, clear2, 0)
    lax.fori_loop(0, parts, clear_counts, 0)

    def fine(i, carry):
        owner = owner_ref[i]
        rank = count_ref[owner]
        count_ref[owner] = rank + 1
        here = (owner ^ dom) * capacity + rank
        there = (owner * capacity + rank) * stencil
        place = place_ref[i]
        source_ref[here] = i
        for k in range(stencil):
            col = cols_ref[k, i]
            step = jnp.where(col < first, 0, jnp.where(col >= first + span, 2, 1))
            begin = ((region + step - 1) * parts + dom) * rows
            near_ref[here * stencil + k] = step * rows + col - begin
            target_ref[there + k] = slot_ref[k, i] * owned + place
        return carry

    lax.fori_loop(0, rows, fine, 0)
    lax.fori_loop(0, parts, clear_counts, 0)

    def coarse(i, carry):
        owner = owner2_ref[i]
        rank = count_ref[owner]
        count_ref[owner] = rank + 1
        source2_ref[(owner ^ dom) * capacity2 + rank] = i
        there = (slots + owner * capacity2 + rank) * stencil
        place = place2_ref[i]
        for k in range(stencil):
            target_ref[there + k] = place * (stencil + 1) + slot2_ref[k, i]
        return carry

    lax.fori_loop(0, rows2, coarse, 0)


def terms_kernel(
    source_ref,
    near_ref,
    blocks_ref,
    before_ref,
    own_ref,
    after_ref,
    *rest,
    offsets,
    capacity,
):
    outs = rest[: len(offsets)]
    table_ref, buffer_ref, table_sem, row_sem = rest[len(offsets) :]
    rows = own_ref.shape[0]
    stencil, width = buffer_ref.shape[1], buffer_ref.shape[2]
    half = width // 2
    narrow = LANES // 2
    flat = narrow * narrow // LANES
    for n, part in enumerate((before_ref, own_ref, after_ref)):
        pltpu.make_async_copy(part, table_ref.at[pl.ds(n * rows, rows)], table_sem.at[n]).start()

    def row_copy(n, slot):
        return pltpu.make_async_copy(blocks_ref.at[source_ref[slot]], buffer_ref.at[n], row_sem.at[n])

    for n, offset in enumerate(offsets):
        for r in range(capacity):
            row_copy(n * capacity + r, offset * capacity + r).start()
    for n, part in enumerate((before_ref, own_ref, after_ref)):
        pltpu.make_async_copy(part, table_ref.at[pl.ds(n * rows, rows)], table_sem.at[n]).wait()

    left = low_lanes((half, LANES), narrow)
    left_flat = low_lanes((flat, LANES), narrow)
    out_row = lax.broadcasted_iota(I32, (narrow, LANES), 0)
    in_col = lax.broadcasted_iota(I32, (narrow, LANES), 1)
    chosen = jnp.where(out_row < flat, 2 * out_row, 2 * (out_row - flat) + 1)
    pick = jnp.where(in_col == chosen, 1.0, 0.0).astype(BF16)
    zero = jnp.zeros((half, LANES), BF16)

    def one_row(n, slot, out_ref, r):
        row_copy(n, slot).wait()
        mine = own_half = table_ref[rows + source_ref[slot]]
        column = jnp.concatenate([mine, pltpu.roll(own_half, narrow, 1)], axis=0)
        turned = lax.dot_general(
            pick, column, (((1,), (1,)), ((), ())), preferred_element_type=F32
        ).astype(BF16)
        products = []
        for k in range(0, stencil, 2):
            one = table_ref[near_ref[slot * stencil + k]]
            weights = [jnp.where(left, one, zero), jnp.where(left, pltpu.roll(one, narrow, 1), zero)]
            lhs = buffer_ref[n, k]
            if k + 1 < stencil:
                two = table_ref[near_ref[slot * stencil + k + 1]]
                weights += [jnp.where(left, zero, pltpu.roll(two, narrow, 1)), jnp.where(left, zero, two)]
                lhs = jnp.concatenate([lhs, buffer_ref[n, k + 1]], axis=1)
            products.append(
                jnp.dot(lhs, jnp.concatenate(weights, axis=0), preferred_element_type=F32).astype(BF16)
            )
        term = jnp.dot(turned, jnp.concatenate(products, axis=1), preferred_element_type=F32)
        for k in range(0, stencil, 2):
            pair = term[:, k // 2 * LANES : (k // 2 + 1) * LANES]
            even = pair[:flat]
            odd = pair[flat:]
            base = (r * stencil + k) * flat
            out_ref[pl.ds(base, flat), :] = jnp.where(left_flat, even, pltpu.roll(odd, narrow, 1)).astype(BF16)
            if k + 1 < stencil:
                out_ref[pl.ds(base + flat, flat), :] = jnp.where(
                    left_flat, pltpu.roll(even, narrow, 1), odd
                ).astype(BF16)

    for n, offset in enumerate(offsets):

        def body(r, carry, n=n, offset=offset):
            one_row(n * capacity + r, offset * capacity + r, outs[n], r)
            return carry

        lax.fori_loop(0, capacity, body, 0)


def level_one(source, near, blocks, before, own, after, offsets, capacity):
    rows, stencil, width, _ = blocks.shape
    narrow = LANES // 2
    flat = narrow * narrow // LANES
    shape = jax.ShapeDtypeStruct((capacity * stencil * flat, LANES), BF16)
    count = len(offsets) * capacity
    return pl.pallas_call(
        functools.partial(terms_kernel, offsets=offsets, capacity=capacity),
        out_shape=tuple(shape for _ in offsets),
        in_specs=[smem(), smem(), hbm(), hbm(), hbm(), hbm()],
        out_specs=tuple(vmem() for _ in offsets),
        scratch_shapes=[
            pltpu.VMEM((3 * rows,) + own.shape[1:], BF16),
            pltpu.VMEM((count, stencil, width, width), BF16),
            pltpu.SemaphoreType.DMA((3,)),
            pltpu.SemaphoreType.DMA((count,)),
        ],
        compiler_params=params(),
    )(source, near, blocks, before, own, after)


def owner_kernel(
    where_ref,
    target_ref,
    source2_ref,
    weights_ref,
    own_ref,
    *rest,
    parts,
    capacity,
    capacity2,
    owned,
    stencil,
):
    arrived = rest[:parts]
    out_ref = rest[parts]
    sends = rest[parts + 1 : 2 * parts + 1]
    (sum_ref,) = rest[2 * parts + 1 :]
    dom = where_ref[1]
    flat = sum_ref.shape[1]
    narrow = LANES // 2
    sum_ref[...] = jnp.zeros(sum_ref.shape, F32)
    for d in range(parts):
        part_ref = arrived[d]

        def add(r, carry, d=d, part_ref=part_ref):
            base = (dom * capacity + r) * stencil
            for k in range(stencil):
                target = target_ref[dom ^ d, base + k]
                value = part_ref[pl.ds((r * stencil + k) * flat, flat), :].astype(F32)

                @pl.when(target >= 0)
                def _():
                    sum_ref[target] += value

            return carry

        lax.fori_loop(0, capacity, add, 0)

    left = low_lanes((flat, LANES), narrow)
    quarter = LANES // 4
    eighth = lax.broadcasted_iota(I32, (8, LANES), 1) // quarter

    for d in range(parts):
        send_ref = sends[d]

        def second(r, carry, d=d, send_ref=send_ref):
            q = source2_ref[d * capacity2 + r]
            rows = []
            for k in range(0, stencil, 2):
                one = sum_ref[k * owned + q].astype(BF16)
                if k + 1 < stencil:
                    two = sum_ref[(k + 1) * owned + q].astype(BF16)
                else:
                    two = jnp.zeros((flat, LANES), BF16)
                even = jnp.where(left, one, pltpu.roll(two, narrow, 1))
                odd = jnp.where(left, pltpu.roll(one, narrow, 1), two)
                rows.append(jnp.concatenate([even, odd], axis=0))
            own = own_ref[q]
            groups = []
            for g in range((stencil + 3) // 4):
                lhs = jnp.concatenate(rows[2 * g : 2 * g + 2], axis=1)
                product = jnp.dot(lhs, weights_ref[q, g], preferred_element_type=F32).astype(BF16)
                groups.append(product)
            term = jnp.dot(own, jnp.concatenate(groups, axis=1), preferred_element_type=F32)
            for k in range(stencil):
                g = k // 4
                total = None
                for w in range(4):
                    piece = term[w * 8 : (w + 1) * 8, g * LANES : (g + 1) * LANES]
                    shift = (w - k) % 4 * quarter
                    if shift:
                        piece = pltpu.roll(piece, shift, 1)
                    total = piece if total is None else jnp.where(eighth == w, piece, total)
                send_ref[pl.ds((r * stencil + k) * 8, 8), :] = total
            return carry

        lax.fori_loop(0, capacity2, second, 0)
    for s in range(stencil * owned):
        out_ref[s] = sum_ref[s].astype(BF16)


def owner_level(where, targets, source2, weights, own, arrived, parts, capacity, capacity2, owned, stencil):
    flat = LANES // 4
    send = jax.ShapeDtypeStruct((capacity2 * stencil * 8, LANES), F32)
    return pl.pallas_call(
        functools.partial(
            owner_kernel, parts=parts, capacity=capacity, capacity2=capacity2, owned=owned, stencil=stencil
        ),
        out_shape=(jax.ShapeDtypeStruct((stencil * owned, flat, LANES), BF16),) + (send,) * parts,
        in_specs=[smem(), smem(), smem()] + [vmem()] * (2 + parts),
        out_specs=(vmem(),) * (1 + parts),
        scratch_shapes=[pltpu.VMEM((stencil * owned, flat, LANES), F32)],
        compiler_params=params(),
    )(where, targets, source2, weights, own, *arrived)


def final_kernel(where_ref, target_ref, *rest, parts, first, capacity2, stencil):
    arrived = rest[:parts]
    out_ref = rest[parts]
    (sum_ref,) = rest[parts + 1 :]
    dom = where_ref[1]
    deep = stencil + 1
    sum_ref[...] = jnp.zeros(sum_ref.shape, F32)
    for d in range(parts):
        for r in range(capacity2):
            base = (first + dom * capacity2 + r) * stencil
            for k in range(stencil):
                target = target_ref[dom ^ d, base + k]
                value = arrived[d][pl.ds((r * stencil + k) * 8, 8), :].astype(F32)

                @pl.when(target >= 0)
                def _(target=target, value=value):
                    sum_ref[pl.ds(target * 8, 8), :] += value

    for u in range(out_ref.shape[0]):
        for t in range(8):
            tile = sum_ref[pl.ds(u * deep * 8 + t, deep, stride=8), :]
            out_ref[u, :, pl.ds(t * LANES, LANES)] = tile[:stencil].astype(BF16)


def final_level(where, targets, arrived, parts, first, capacity2, owned2, stencil):
    return pl.pallas_call(
        functools.partial(final_kernel, parts=parts, first=first, capacity2=capacity2, stencil=stencil),
        out_shape=jax.ShapeDtypeStruct((owned2, stencil, 8 * LANES), BF16),
        in_specs=[smem(), smem()] + [vmem()] * parts,
        out_specs=vmem(),
        scratch_shapes=[pltpu.VMEM((owned2 * (stencil + 1) * 8, LANES), F32)],
        compiler_params=params(),
    )(where, targets, *arrived)


def chunks_of(parts):
    order = list(range(parts - 1, -1, -1))
    return [tuple(order[i : i + 2]) for i in range(0, parts, 2)]


def local(
    fine_blocks,
    interp,
    fine_cols,
    fine_slot,
    fine_owner,
    fine_place,
    coarse_interp,
    coarse_cols,
    coarse_slot,
    coarse_owner,
    coarse_place,
):
    rows, stencil, width, _ = fine_blocks.shape
    narrow = interp.shape[1] // width
    narrow2 = coarse_interp.shape[1] // narrow
    parts = lax.axis_size("dom")
    region = lax.axis_index("region")
    dom = lax.axis_index("dom")
    owned = rows // 2
    owned2 = owned // 2
    capacity = max(2, rows // 8)
    capacity2 = max(2, owned // 8)
    slots = parts * capacity
    slots2 = parts * capacity2
    where = jnp.stack([region, dom]).astype(I32)

    coarse_before, coarse_after = neighbours(coarse_interp, "region")
    own = halves(interp)
    before, after = neighbours(own, "region")

    source, near, target, source2 = pl.pallas_call(
        functools.partial(
            index_kernel, parts=parts, capacity=capacity, capacity2=capacity2, owned=owned, owned2=owned2
        ),
        out_shape=(
            jax.ShapeDtypeStruct((slots,), I32),
            jax.ShapeDtypeStruct((slots * stencil,), I32),
            jax.ShapeDtypeStruct(((slots + slots2) * stencil,), I32),
            jax.ShapeDtypeStruct((slots2,), I32),
        ),
        in_specs=[smem()] * 8,
        out_specs=(smem(),) * 4,
        scratch_shapes=[pltpu.SMEM((parts,), I32)],
    )(
        where,
        fine_cols.T,
        fine_slot.T,
        fine_owner[:, 0],
        fine_place,
        coarse_slot.T,
        coarse_owner[:, 0],
        coarse_place,
    )

    size2 = coarse_interp.shape[1]
    extra = 8 * pl.cdiv(target.shape[0], 8 * size2)
    codes = jnp.pad(target, (0, extra * size2 - target.shape[0])).astype(BF16).reshape(extra, size2)
    stacked = jnp.concatenate([coarse_before, coarse_interp, coarse_after, codes], axis=0)
    collected = lax.all_gather(stacked, "dom", axis=0, tiled=False)
    targets = collected[:, 3 * owned :].reshape(parts, extra * size2)[:, : target.shape[0]].astype(I32)
    span2 = parts * owned
    inside = coarse_cols % span2
    index2 = (inside // owned) * (3 * owned + extra) + (coarse_cols // span2 - region + 1) * owned + inside % owned
    picked = collected.reshape(parts * (3 * owned + extra), size2)[index2.reshape(-1)]
    picked = picked.reshape(owned, stencil, narrow, narrow2)
    groups = (stencil + 3) // 4
    picked = jnp.pad(picked, ((0, 0), (0, 4 * groups - stencil), (0, 0), (0, 0)))
    picked = picked.reshape(owned, groups, 4, narrow, 1, narrow2)
    corner = jnp.eye(4, dtype=jnp.bool_).reshape(1, 1, 4, 1, 4, 1)
    weights = jnp.where(corner, picked, jnp.zeros((), BF16)).reshape(owned, groups, 4 * narrow, 4 * narrow2)
    turned = coarse_interp.reshape(owned, narrow // 2, 2, narrow2 // 4, 4)
    turned = turned.transpose(0, 4, 3, 2, 1).reshape(owned, narrow2, narrow)

    arrived = [None] * parts
    for offsets in chunks_of(parts):
        sent = level_one(source, near, fine_blocks, before, own, after, offsets, capacity)
        for offset, cells in zip(offsets, sent):
            arrived[offset] = exchange(cells, "dom", offset) if offset else cells
    outs = owner_level(
        where, targets, source2, weights, turned, arrived, parts, capacity, capacity2, owned, stencil
    )
    coarse_blocks = outs[0].reshape(stencil, owned, narrow * narrow).transpose(1, 0, 2)
    arrived2 = [exchange(cells.astype(BF16), "dom", d) if d else cells for d, cells in enumerate(outs[1:])]
    second = final_level(where, targets, arrived2, parts, slots, capacity2, owned2, stencil)
    return (coarse_blocks, second)


def solution(mesh):
    in_specs = (
        P(("region", "dom"), None, None, None),
        P(("region", "dom"), None),
        P(("region", "dom"), None),
        P(("region", "dom"), None),
        P(("region", "dom"), None),
        P(("region", "dom")),
        P(("region", "dom"), None),
        P(("region", "dom"), None),
        P(("region", "dom"), None),
        P(("region", "dom"), None),
        P(("region", "dom")),
    )
    out_specs = (P(("region", "dom"), None, None), P(("region", "dom"), None, None))
    return jax.shard_map(local, mesh=mesh, in_specs=in_specs, out_specs=out_specs, check_vma=False)
```

```python
import functools

import jax
import jax.numpy as jnp
from jax import lax
from jax.experimental import pallas as pl
from jax.experimental.pallas import tpu as pltpu
from jax.sharding import PartitionSpec as P

BF16 = jnp.bfloat16
F32 = jnp.float32
I32 = jnp.int32
LANES = 128
VMEM_LIMIT = 48 * 1024 * 1024


def vmem():
    return pl.BlockSpec(memory_space=pltpu.VMEM)


def smem():
    return pl.BlockSpec(memory_space=pltpu.SMEM)


def hbm():
    return pl.BlockSpec(memory_space=pl.ANY)


def params():
    return pltpu.CompilerParams(vmem_limit_bytes=VMEM_LIMIT)


def low_lanes(shape, bound):
    return lax.broadcasted_iota(I32, shape, len(shape) - 1) < bound


def exchange(cells, axis, offset):
    count = lax.axis_size(axis)
    return lax.ppermute(cells, axis, [(i, i ^ offset) for i in range(count)])


def neighbours(cells, axis):
    count = lax.axis_size(axis)
    previous = lax.ppermute(cells, axis, [(i, i + 1) for i in range(count - 1)])
    following = lax.ppermute(cells, axis, [(i + 1, i) for i in range(count - 1)])
    return previous, following


def halves_kernel(flat_ref, coarse_ref, out_ref, quarters_ref, wide_ref):
    group = flat_ref.shape[0]
    deep = flat_ref.shape[1] // LANES
    half = deep // 2
    left = low_lanes((group, LANES), LANES // 2)
    for t in range(half):
        upper = flat_ref[:, pl.ds(t * LANES, LANES)].astype(F32)
        lower = flat_ref[:, pl.ds((t + half) * LANES, LANES)].astype(F32)
        even = jnp.where(left, upper, pltpu.roll(lower, LANES // 2, 1))
        odd = jnp.where(left, pltpu.roll(upper, LANES // 2, 1), lower)
        wide_ref[pl.ds(2 * t, group, stride=deep), :] = even
        wide_ref[pl.ds(2 * t + 1, group, stride=deep), :] = odd
    for r in range(group):
        out_ref[r] = wide_ref[pl.ds(r * deep, deep), :].astype(BF16)
    count = coarse_ref.shape[0]
    deep2 = coarse_ref.shape[1] // LANES
    quarter = LANES // 4
    lane = lax.broadcasted_iota(I32, (count, LANES), 1) // quarter
    for t in range(deep2 // 4):
        tiles = [coarse_ref[:, pl.ds((h * deep2 // 4 + t) * LANES, LANES)].astype(F32) for h in range(4)]
        for u in range(4):
            total = None
            for h in range(4):
                shift = (h - u) % 4 * quarter
                piece = pltpu.roll(tiles[h], shift, 1) if shift else tiles[h]
                total = piece if total is None else jnp.where(lane == h, piece, total)
            wide_ref[pl.ds(4 * t + u, count, stride=deep2), :] = total
    for r in range(count):
        quarters_ref[r] = wide_ref[pl.ds(r * deep2, deep2), :].astype(BF16)


def halves(flat, coarse):
    rows, size = flat.shape
    count, size2 = coarse.shape
    deep = size // LANES
    deep2 = size2 // LANES
    group = 16
    steps = rows // group
    group2 = count // steps
    return pl.pallas_call(
        halves_kernel,
        grid=(steps,),
        out_shape=(
            jax.ShapeDtypeStruct((rows, deep, LANES), BF16),
            jax.ShapeDtypeStruct((count, deep2, LANES), BF16),
        ),
        in_specs=[
            pl.BlockSpec((group, size), lambda i: (i, 0)),
            pl.BlockSpec((group2, size2), lambda i: (i, 0)),
        ],
        out_specs=(
            pl.BlockSpec((group, deep, LANES), lambda i: (i, 0, 0)),
            pl.BlockSpec((group2, deep2, LANES), lambda i: (i, 0, 0)),
        ),
        scratch_shapes=[pltpu.VMEM((group * deep, LANES), F32)],
        compiler_params=params(),
    )(flat, coarse)


def index_kernel(
    where_ref,
    cols_ref,
    slot_ref,
    owner_ref,
    place_ref,
    slot2_ref,
    owner2_ref,
    place2_ref,
    plan_ref,
    target_ref,
    count_ref,
    *,
    parts,
    capacity,
    capacity2,
    owned,
    owned2,
):
    region = where_ref[0]
    dom = where_ref[1]
    stencil, rows = cols_ref.shape
    rows2 = slot2_ref.shape[1]
    span = parts * rows
    first = region * span
    slots = parts * capacity
    slots2 = parts * capacity2
    second = slots * (stencil + 1)

    def clear_counts(d, carry):
        count_ref[d] = 0
        return carry

    if slots > rows or slots2 > rows2:

        def clear(p, carry):
            plan_ref[p] = 0
            for k in range(stencil):
                plan_ref[slots + p * stencil + k] = 1
                target_ref[p * stencil + k] = stencil * owned
            return carry

        lax.fori_loop(0, slots, clear, 0)

        def clear2(p, carry):
            plan_ref[second + p] = 0
            for k in range(stencil):
                target_ref[(slots + p) * stencil + k] = (stencil + 1) * owned2
            return carry

        lax.fori_loop(0, slots2, clear2, 0)
    lax.fori_loop(0, parts, clear_counts, 0)

    def fine(i, carry):
        owner = owner_ref[i]
        rank = count_ref[owner]
        count_ref[owner] = rank + 1
        here = (owner ^ dom) * capacity + rank
        there = (owner * capacity + rank) * stencil
        place = place_ref[i]
        plan_ref[here] = i
        for k in range(stencil):
            col = cols_ref[k, i]
            step = jnp.where(col < first, 0, jnp.where(col >= first + span, 2, 1))
            begin = ((region + step - 1) * parts + dom) * rows
            plan_ref[slots + here * stencil + k] = (col - begin) * 4 + step
            target_ref[there + k] = slot_ref[k, i] * owned + place
        return carry

    lax.fori_loop(0, rows, fine, 0)
    lax.fori_loop(0, parts, clear_counts, 0)

    def coarse(i, carry):
        owner = owner2_ref[i]
        rank = count_ref[owner]
        count_ref[owner] = rank + 1
        plan_ref[second + (owner ^ dom) * capacity2 + rank] = i
        there = (slots + owner * capacity2 + rank) * stencil
        place = place2_ref[i]
        for k in range(stencil):
            target_ref[there + k] = place * (stencil + 1) + slot2_ref[k, i]
        return carry

    lax.fori_loop(0, rows2, coarse, 0)


def terms_kernel(plan_ref, blocks_ref, before_ref, own_ref, after_ref, *rest, offsets, capacity, slots):
    outs = rest[: len(offsets)]
    buffer_ref, row_sem = rest[len(offsets) :]
    stencil, width = buffer_ref.shape[1], buffer_ref.shape[2]
    half = width // 2
    narrow = LANES // 2
    flat = narrow * narrow // LANES

    def row_copy(n, slot):
        return pltpu.make_async_copy(blocks_ref.at[plan_ref[slot]], buffer_ref.at[n], row_sem.at[n])

    for n, offset in enumerate(offsets):
        for r in range(capacity):
            row_copy(n * capacity + r, offset * capacity + r).start()

    left = low_lanes((half, LANES), narrow)
    left_flat = low_lanes((flat, LANES), narrow)
    out_row = lax.broadcasted_iota(I32, (narrow, LANES), 0)
    in_col = lax.broadcasted_iota(I32, (narrow, LANES), 1)
    chosen = jnp.where(out_row < flat, 2 * out_row, 2 * (out_row - flat) + 1)
    pick = jnp.where(in_col == chosen, 1.0, 0.0).astype(BF16)
    zero = jnp.zeros((half, LANES), BF16)

    def neighbour(slot, k):
        code = plan_ref[slots + slot * stencil + k]
        row = lax.shift_right_logical(code, 2)
        step = code & 3
        return jnp.where(step == 0, before_ref[row], jnp.where(step == 1, own_ref[row], after_ref[row]))

    def one_row(n, slot, out_ref, r):
        mine = own_ref[plan_ref[slot]]
        column = jnp.concatenate([mine, pltpu.roll(mine, narrow, 1)], axis=0)
        turned = lax.dot_general(
            pick, column, (((1,), (1,)), ((), ())), preferred_element_type=F32
        ).astype(BF16)
        products = []
        for k in range(0, stencil, 2):
            one = neighbour(slot, k)
            weights = [jnp.where(left, one, zero), jnp.where(left, pltpu.roll(one, narrow, 1), zero)]
            lhs = buffer_ref[n, k]
            if k + 1 < stencil:
                two = neighbour(slot, k + 1)
                weights += [jnp.where(left, zero, pltpu.roll(two, narrow, 1)), jnp.where(left, zero, two)]
                lhs = jnp.concatenate([lhs, buffer_ref[n, k + 1]], axis=1)
            products.append(
                jnp.dot(lhs, jnp.concatenate(weights, axis=0), preferred_element_type=F32).astype(BF16)
            )
        term = jnp.dot(turned, jnp.concatenate(products, axis=1), preferred_element_type=F32)
        for k in range(0, stencil, 2):
            pair = term[:, k // 2 * LANES : (k // 2 + 1) * LANES]
            even = pair[:flat]
            odd = pair[flat:]
            base = (r * stencil + k) * flat
            out_ref[pl.ds(base, flat), :] = jnp.where(left_flat, even, pltpu.roll(odd, narrow, 1)).astype(BF16)
            if k + 1 < stencil:
                out_ref[pl.ds(base + flat, flat), :] = jnp.where(
                    left_flat, pltpu.roll(even, narrow, 1), odd
                ).astype(BF16)

    for n, offset in enumerate(offsets):
        for r in range(capacity):
            row_copy(n * capacity + r, offset * capacity + r).wait()
        for r in range(capacity):
            one_row(n * capacity + r, offset * capacity + r, outs[n], r)


def level_one(plan, blocks, before, own, after, offsets, capacity, slots):
    rows, stencil, width, _ = blocks.shape
    narrow = LANES // 2
    flat = narrow * narrow // LANES
    shape = jax.ShapeDtypeStruct((capacity * stencil * flat, LANES), BF16)
    count = len(offsets) * capacity
    return pl.pallas_call(
        functools.partial(terms_kernel, offsets=offsets, capacity=capacity, slots=slots),
        out_shape=tuple(shape for _ in offsets),
        in_specs=[smem(), hbm(), vmem(), vmem(), vmem()],
        out_specs=tuple(vmem() for _ in offsets),
        scratch_shapes=[
            pltpu.VMEM((count, stencil, width, width), BF16),
            pltpu.SemaphoreType.DMA((count,)),
        ],
        compiler_params=params(),
    )(plan, blocks, before, own, after)


def pick_kernel(index_ref, before_ref, own_ref, after_ref, out_ref):
    stencil, count = index_ref.shape

    def body(q, carry):
        for k in range(stencil):
            code = index_ref[k, q]
            row = lax.shift_right_logical(code, 2)
            step = code & 3
            out_ref[q * stencil + k] = jnp.where(
                step == 0, before_ref[row], jnp.where(step == 1, own_ref[row], after_ref[row])
            )
        return carry

    lax.fori_loop(0, count, body, 0, unroll=4)


def pick_rows(index, before, own, after):
    stencil, count = index.shape
    return pl.pallas_call(
        pick_kernel,
        out_shape=jax.ShapeDtypeStruct((count * stencil,) + own.shape[1:], own.dtype),
        in_specs=[smem(), vmem(), vmem(), vmem()],
        out_specs=vmem(),
        compiler_params=params(),
    )(index, before, own, after)


def owner_kernel(
    where_ref,
    target_ref,
    plan_ref,
    picked_ref,
    own_ref,
    *rest,
    parts,
    capacity,
    capacity2,
    owned,
    stencil,
):
    arrived = rest[:parts]
    out_ref = rest[parts]
    sends = rest[parts + 1 : 2 * parts + 1]
    sum_ref, term_ref = rest[2 * parts + 1 :]
    dom = where_ref[1]
    second_slot = parts * capacity * (stencil + 1)
    flat = sum_ref.shape[1]
    narrow = LANES // 2
    sum_ref[...] = jnp.zeros(sum_ref.shape, F32)
    for d in range(parts):
        part_ref = arrived[d]

        def add(r, carry, d=d, part_ref=part_ref):
            base = (dom * capacity + r) * stencil
            for k in range(stencil):
                target = target_ref[dom ^ d, base + k]
                sum_ref[target] += part_ref[pl.ds((r * stencil + k) * flat, flat), :].astype(F32)
            return carry

        lax.fori_loop(0, capacity, add, 0, unroll=True)

    left = low_lanes((flat, LANES), narrow)
    quarter = LANES // 4
    eighth = lax.broadcasted_iota(I32, (8, LANES), 1) // quarter
    block = lax.broadcasted_iota(I32, (16, LANES), 1) // quarter
    none = jnp.zeros((16, LANES), BF16)

    def second(d, carry):
        for r in range(capacity2):
            q = plan_ref[second_slot + d * capacity2 + r]
            rows = []
            weights = []
            for k in range(0, stencil, 2):
                one = sum_ref[k * owned + q].astype(BF16)
                out_ref[k * owned + q] = one
                if k + 1 < stencil:
                    two = sum_ref[(k + 1) * owned + q].astype(BF16)
                    out_ref[(k + 1) * owned + q] = two
                else:
                    two = jnp.zeros((flat, LANES), BF16)
                even = jnp.where(left, one, pltpu.roll(two, narrow, 1))
                odd = jnp.where(left, pltpu.roll(one, narrow, 1), two)
                rows.append(jnp.concatenate([even, odd], axis=0))
            for k in range(stencil):
                packed = picked_ref[q * stencil + k]
                for h in range(4):
                    shift = (k - h) % 4 * quarter
                    turned = pltpu.roll(packed, shift, 1) if shift else packed
                    weights.append(jnp.where(block == k % 4, turned, none))
            own = own_ref[q]
            groups = []
            for g in range((stencil + 3) // 4):
                lhs = jnp.concatenate(rows[2 * g : 2 * g + 2], axis=1)
                rhs = jnp.concatenate(weights[16 * g : 16 * g + 16], axis=0)
                product = jnp.dot(lhs[:, : rhs.shape[0]], rhs, preferred_element_type=F32)
                groups.append(product.astype(BF16))
            term = jnp.dot(own, jnp.concatenate(groups, axis=1), preferred_element_type=F32)
            for k in range(stencil):
                g = k // 4
                total = None
                for w in range(4):
                    piece = term[w * 8 : (w + 1) * 8, g * LANES : (g + 1) * LANES]
                    shift = (w - k) % 4 * quarter
                    if shift:
                        piece = pltpu.roll(piece, shift, 1)
                    total = piece if total is None else jnp.where(eighth == w, piece, total)
                term_ref[d, pl.ds((r * stencil + k) * 8, 8), :] = total
        return carry

    lax.fori_loop(0, parts, second, 0, unroll=4)
    for d in range(parts):
        sends[d][...] = term_ref[d].astype(BF16)


def owner_level(where, targets, plan, picked, own, arrived, parts, capacity, capacity2, owned, stencil):
    flat = LANES // 4
    send = jax.ShapeDtypeStruct((capacity2 * stencil * 8, LANES), BF16)
    return pl.pallas_call(
        functools.partial(
            owner_kernel, parts=parts, capacity=capacity, capacity2=capacity2, owned=owned, stencil=stencil
        ),
        out_shape=(jax.ShapeDtypeStruct((stencil * owned, flat, LANES), BF16),) + (send,) * parts,
        in_specs=[smem(), smem(), smem()] + [vmem()] * (2 + parts),
        out_specs=(vmem(),) * (1 + parts),
        scratch_shapes=[
            pltpu.VMEM((stencil * owned + 1, flat, LANES), F32),
            pltpu.VMEM((parts, capacity2 * stencil * 8, LANES), F32),
        ],
        compiler_params=params(),
    )(where, targets, plan, picked, own, *arrived)


def final_kernel(where_ref, target_ref, *rest, parts, first, capacity2, stencil):
    arrived = rest[:parts]
    out_ref = rest[parts]
    (sum_ref,) = rest[parts + 1 :]
    dom = where_ref[1]
    deep = stencil + 1
    sum_ref[...] = jnp.zeros(sum_ref.shape, F32)
    for d in range(parts):
        values = arrived[d][...].astype(F32)
        for r in range(capacity2):
            base = (first + dom * capacity2 + r) * stencil
            for k in range(stencil):
                at = r * stencil + k
                sum_ref[target_ref[dom ^ d, base + k]] += values[at * 8 : (at + 1) * 8]
    for u in range(out_ref.shape[0]):
        for t in range(8):
            tile = sum_ref[pl.ds(u * deep, deep), t, :]
            out_ref[u, :, pl.ds(t * LANES, LANES)] = tile[:stencil].astype(BF16)


def final_level(where, targets, arrived, parts, first, capacity2, owned2, stencil):
    return pl.pallas_call(
        functools.partial(final_kernel, parts=parts, first=first, capacity2=capacity2, stencil=stencil),
        out_shape=jax.ShapeDtypeStruct((owned2, stencil, 8 * LANES), BF16),
        in_specs=[smem(), smem()] + [vmem()] * parts,
        out_specs=vmem(),
        scratch_shapes=[pltpu.VMEM((owned2 * (stencil + 1) + 1, 8, LANES), F32)],
        compiler_params=params(),
    )(where, targets, *arrived)


def chunks_of(parts):
    order = list(range(parts - 1, -1, -1))
    return [(order[0],)] + [tuple(order[i : i + 2]) for i in range(1, parts - 1, 2)] + [(order[-1],)]


def local(
    fine_blocks,
    interp,
    fine_cols,
    fine_slot,
    fine_owner,
    fine_place,
    coarse_interp,
    coarse_cols,
    coarse_slot,
    coarse_owner,
    coarse_place,
):
    rows, stencil, width, _ = fine_blocks.shape
    narrow = interp.shape[1] // width
    narrow2 = coarse_interp.shape[1] // narrow
    parts = lax.axis_size("dom")
    region = lax.axis_index("region")
    dom = lax.axis_index("dom")
    owned = rows // 2
    owned2 = owned // 2
    capacity = max(2, rows // 8)
    capacity2 = max(2, owned // 8)
    slots = parts * capacity
    slots2 = parts * capacity2
    where = jnp.stack([region, dom]).astype(I32)

    own, quarters = halves(interp, coarse_interp)
    before, after = neighbours(own, "region")

    plan, target = pl.pallas_call(
        functools.partial(
            index_kernel, parts=parts, capacity=capacity, capacity2=capacity2, owned=owned, owned2=owned2
        ),
        out_shape=(
            jax.ShapeDtypeStruct((slots * (stencil + 1) + slots2,), I32),
            jax.ShapeDtypeStruct(((slots + slots2) * stencil,), I32),
        ),
        in_specs=[smem()] * 8,
        out_specs=(smem(),) * 2,
        scratch_shapes=[pltpu.SMEM((parts,), I32)],
    )(
        where,
        fine_cols.T,
        fine_slot.T,
        fine_owner[:, 0],
        fine_place,
        coarse_slot.T,
        coarse_owner[:, 0],
        coarse_place,
    )

    size2 = coarse_interp.shape[1]
    extra = pl.cdiv(target.shape[0], size2)
    codes = jnp.pad(target, (0, extra * size2 - target.shape[0])).astype(BF16)
    stacked = jnp.concatenate([quarters, codes.reshape((extra,) + quarters.shape[1:])], axis=0)
    table = lax.all_gather(stacked, "dom", axis=0, tiled=True)
    table_before, table_after = neighbours(table, "region")
    pitch = owned + extra
    targets = table.reshape((parts, pitch) + quarters.shape[1:])[:, owned:].reshape(parts, extra * size2)
    targets = targets[:, : target.shape[0]].astype(I32)
    span2 = parts * owned
    inside = coarse_cols % span2
    index2 = (inside // owned * pitch + inside % owned) * 4 + coarse_cols // span2 - region + 1
    picked = pick_rows(index2.T, table_before, table, table_after)
    turned = coarse_interp.reshape(owned, narrow // 2, 2, narrow2 // 4, 4)
    turned = turned.transpose(0, 4, 3, 2, 1).reshape(owned, narrow2, narrow)

    arrived = [None] * parts
    for offsets in chunks_of(parts):
        sent = level_one(plan, fine_blocks, before, own, after, offsets, capacity, slots)
        for offset, cells in zip(offsets, sent):
            arrived[offset] = exchange(cells, "dom", offset) if offset else cells
    outs = owner_level(
        where, targets, plan, picked, turned, arrived, parts, capacity, capacity2, owned, stencil
    )
    coarse_blocks = outs[0].reshape(stencil, owned, narrow * narrow).transpose(1, 0, 2)
    arrived2 = [exchange(cells, "dom", d) if d else cells for d, cells in enumerate(outs[1:])]
    second = final_level(where, targets, arrived2, parts, slots, capacity2, owned2, stencil)
    return (coarse_blocks, second)


def solution(mesh):
    in_specs = (
        P(("region", "dom"), None, None, None),
        P(("region", "dom"), None),
        P(("region", "dom"), None),
        P(("region", "dom"), None),
        P(("region", "dom"), None),
        P(("region", "dom")),
        P(("region", "dom"), None),
        P(("region", "dom"), None),
        P(("region", "dom"), None),
        P(("region", "dom"), None),
        P(("region", "dom")),
    )
    out_specs = (P(("region", "dom"), None, None), P(("region", "dom"), None, None))
    return jax.shard_map(local, mesh=mesh, in_specs=in_specs, out_specs=out_specs, check_vma=False)
```

```python
import functools

import jax
import jax.numpy as jnp
from jax import lax
from jax.experimental import pallas as pl
from jax.experimental.pallas import tpu as pltpu
from jax.sharding import PartitionSpec as P

BF16 = jnp.bfloat16
F32 = jnp.float32
I32 = jnp.int32
LANES = 128
VMEM_LIMIT = 32 * 1024 * 1024


def vmem():
    return pl.BlockSpec(memory_space=pltpu.VMEM)


def smem():
    return pl.BlockSpec(memory_space=pltpu.SMEM)


def hbm():
    return pl.BlockSpec(memory_space=pl.ANY)


def params():
    return pltpu.CompilerParams(vmem_limit_bytes=VMEM_LIMIT)


def low_lanes(shape, bound):
    return lax.broadcasted_iota(I32, shape, len(shape) - 1) < bound


def exchange(cells, axis, offset):
    count = lax.axis_size(axis)
    return lax.ppermute(cells, axis, [(i, i ^ offset) for i in range(count)])


def partner(index, odd, count):
    other = ((index + odd) ^ 1) - odd
    return other if 0 <= other < count else index


def neighbours(cells, axis):
    count = lax.axis_size(axis)
    return tuple(lax.ppermute(cells, axis, [(i, partner(i, odd, count)) for i in range(count)]) for odd in (0, 1))


def table_of(step, region):
    swapped = jnp.where(region % 2 == 0, 2 - step, step)
    return jnp.where(step == 1, 1, swapped)


def halves_kernel(flat_ref, out_ref, rows_ref, wide_ref, sems):
    steps, group = rows_ref.shape[:2]
    deep = rows_ref.shape[2] // LANES
    half = deep // 2
    left = low_lanes((group, LANES), LANES // 2)

    def copy(g):
        return pltpu.make_async_copy(flat_ref.at[pl.ds(g * group, group)], rows_ref.at[g], sems.at[g])

    for g in range(steps):
        copy(g).start()
    for g in range(steps):
        copy(g).wait()
        for t in range(half):
            upper = rows_ref[g, :, pl.ds(t * LANES, LANES)].astype(F32)
            lower = rows_ref[g, :, pl.ds((t + half) * LANES, LANES)].astype(F32)
            even = jnp.where(left, upper, pltpu.roll(lower, LANES // 2, 1))
            odd = jnp.where(left, pltpu.roll(upper, LANES // 2, 1), lower)
            wide_ref[g, pl.ds(2 * t, group, stride=deep), :] = even
            wide_ref[g, pl.ds(2 * t + 1, group, stride=deep), :] = odd
        for r in range(group):
            out_ref[g * group + r] = wide_ref[g, pl.ds(r * deep, deep), :].astype(BF16)


def halves(flat):
    rows, size = flat.shape
    deep = size // LANES
    group = 16
    steps = rows // group
    return pl.pallas_call(
        halves_kernel,
        out_shape=jax.ShapeDtypeStruct((rows, deep, LANES), BF16),
        in_specs=[pl.BlockSpec(memory_space=pltpu.HBM)],
        out_specs=vmem(),
        scratch_shapes=[
            pltpu.VMEM((steps, group, size), BF16),
            pltpu.VMEM((steps, group * deep, LANES), F32),
            pltpu.SemaphoreType.DMA((steps,)),
        ],
        compiler_params=params(),
    )(pltpu.with_memory_space_constraint(flat, pltpu.HBM))


def quarters_of(coarse_ref, quarters_ref, wide_ref):
    count = coarse_ref.shape[0]
    deep = coarse_ref.shape[1] // LANES
    quarter = LANES // 4
    lane = lax.broadcasted_iota(I32, (count, LANES), 1) // quarter
    for t in range(deep // 4):
        tiles = [coarse_ref[:, pl.ds((h * deep // 4 + t) * LANES, LANES)].astype(F32) for h in range(4)]
        for u in range(4):
            total = None
            for h in range(4):
                shift = (h - u) % 4 * quarter
                piece = pltpu.roll(tiles[h], shift, 1) if shift else tiles[h]
                total = piece if total is None else jnp.where(lane == h, piece, total)
            wide_ref[pl.ds(4 * t + u, count, stride=deep), :] = total
    for r in range(count):
        quarters_ref[r] = wide_ref[pl.ds(r * deep, deep), :].astype(BF16)


def index_kernel(
    where_ref,
    cols_ref,
    slot_ref,
    owner_ref,
    place_ref,
    slot2_ref,
    owner2_ref,
    place2_ref,
    coarse_ref,
    plan_ref,
    target_ref,
    quarters_ref,
    count_ref,
    wide_ref,
    *,
    parts,
    capacity,
    capacity2,
    owned,
    owned2,
):
    quarters_of(coarse_ref, quarters_ref, wide_ref)
    region = where_ref[0]
    dom = where_ref[1]
    stencil, rows = cols_ref.shape
    rows2 = slot2_ref.shape[1]
    span = parts * rows
    first = region * span
    slots = parts * capacity
    slots2 = parts * capacity2
    second = slots * (stencil + 1)

    def clear_counts(d, carry):
        count_ref[d] = 0
        return carry

    if slots > rows or slots2 > rows2:

        def clear(p, carry):
            plan_ref[p] = 0
            for k in range(stencil):
                plan_ref[slots + p * stencil + k] = 1
                target_ref[p * stencil + k] = stencil * owned
            return carry

        lax.fori_loop(0, slots, clear, 0)

        def clear2(p, carry):
            plan_ref[second + p] = 0
            for k in range(stencil):
                target_ref[(slots + p) * stencil + k] = (stencil + 1) * owned2
            return carry

        lax.fori_loop(0, slots2, clear2, 0)
    lax.fori_loop(0, parts, clear_counts, 0)

    def fine(i, carry):
        owner = owner_ref[i]
        rank = count_ref[owner]
        count_ref[owner] = rank + 1
        here = (owner ^ dom) * capacity + rank
        there = (owner * capacity + rank) * stencil
        place = place_ref[i]
        plan_ref[here] = i
        for k in range(stencil):
            col = cols_ref[k, i]
            step = jnp.where(col < first, 0, jnp.where(col >= first + span, 2, 1))
            begin = ((region + step - 1) * parts + dom) * rows
            plan_ref[slots + here * stencil + k] = (col - begin) * 4 + table_of(step, region)
            target_ref[there + k] = slot_ref[k, i] * owned + place
        return carry

    lax.fori_loop(0, rows, fine, 0)
    lax.fori_loop(0, parts, clear_counts, 0)

    def coarse(i, carry):
        owner = owner2_ref[i]
        rank = count_ref[owner]
        count_ref[owner] = rank + 1
        plan_ref[second + (owner ^ dom) * capacity2 + rank] = i
        there = (slots + owner * capacity2 + rank) * stencil
        place = place2_ref[i]
        for k in range(stencil):
            target_ref[there + k] = place * (stencil + 1) + slot2_ref[k, i]
        return carry

    lax.fori_loop(0, rows2, coarse, 0)


def terms_kernel(plan_ref, blocks_ref, before_ref, own_ref, after_ref, *rest, offsets, capacity, slots, waited):
    outs = rest[waited : waited + len(offsets)]
    buffer_ref, row_sem = rest[waited + len(offsets) :]
    stencil, width = buffer_ref.shape[1], buffer_ref.shape[2]
    half = width // 2
    narrow = LANES // 2
    flat = narrow * narrow // LANES

    def row_copy(n, slot):
        return pltpu.make_async_copy(blocks_ref.at[plan_ref[slot]], buffer_ref.at[n], row_sem.at[n])

    for n, offset in enumerate(offsets):
        for r in range(capacity):
            row_copy(n * capacity + r, offset * capacity + r).start()

    left = low_lanes((half, LANES), narrow)
    left_flat = low_lanes((flat, LANES), narrow)
    out_row = lax.broadcasted_iota(I32, (narrow, LANES), 0)
    in_col = lax.broadcasted_iota(I32, (narrow, LANES), 1)
    chosen = jnp.where(out_row < flat, 2 * out_row, 2 * (out_row - flat) + 1)
    pick = jnp.where(in_col == chosen, 1.0, 0.0).astype(BF16)
    zero = jnp.zeros((half, LANES), BF16)

    def neighbour(slot, k):
        code = plan_ref[slots + slot * stencil + k]
        row = lax.shift_right_logical(code, 2)
        step = code & 3
        return jnp.where(step == 0, before_ref[row], jnp.where(step == 1, own_ref[row], after_ref[row]))

    def one_row(n, slot, out_ref, r):
        mine = own_ref[plan_ref[slot]]
        column = jnp.concatenate([mine, pltpu.roll(mine, narrow, 1)], axis=0)
        turned = lax.dot_general(
            pick, column, (((1,), (1,)), ((), ())), preferred_element_type=F32
        ).astype(BF16)
        products = []
        for k in range(0, stencil, 2):
            one = neighbour(slot, k)
            weights = [jnp.where(left, one, zero), jnp.where(left, pltpu.roll(one, narrow, 1), zero)]
            lhs = buffer_ref[n, k]
            if k + 1 < stencil:
                two = neighbour(slot, k + 1)
                weights += [jnp.where(left, zero, pltpu.roll(two, narrow, 1)), jnp.where(left, zero, two)]
                lhs = jnp.concatenate([lhs, buffer_ref[n, k + 1]], axis=1)
            products.append(
                jnp.dot(lhs, jnp.concatenate(weights, axis=0), preferred_element_type=F32).astype(BF16)
            )
        term = jnp.dot(turned, jnp.concatenate(products, axis=1), preferred_element_type=F32)
        for k in range(0, stencil, 2):
            pair = term[:, k // 2 * LANES : (k // 2 + 1) * LANES]
            even = pair[:flat]
            odd = pair[flat:]
            base = (r * stencil + k) * flat
            out_ref[pl.ds(base, flat), :] = jnp.where(left_flat, even, pltpu.roll(odd, narrow, 1)).astype(BF16)
            if k + 1 < stencil:
                out_ref[pl.ds(base + flat, flat), :] = jnp.where(
                    left_flat, pltpu.roll(even, narrow, 1), odd
                ).astype(BF16)

    for n, offset in enumerate(offsets):
        for r in range(capacity):
            row_copy(n * capacity + r, offset * capacity + r).wait()
        for r in range(capacity):
            one_row(n * capacity + r, offset * capacity + r, outs[n], r)


def level_one(plan, blocks, before, own, after, offsets, capacity, slots, waited):
    rows, stencil, width, _ = blocks.shape
    narrow = LANES // 2
    flat = narrow * narrow // LANES
    shape = jax.ShapeDtypeStruct((capacity * stencil * flat, LANES), BF16)
    count = len(offsets) * capacity
    return pl.pallas_call(
        functools.partial(terms_kernel, offsets=offsets, capacity=capacity, slots=slots, waited=len(waited)),
        out_shape=tuple(shape for _ in offsets),
        in_specs=[smem(), hbm(), vmem(), vmem(), vmem()] + [hbm()] * len(waited),
        out_specs=tuple(vmem() for _ in offsets),
        scratch_shapes=[
            pltpu.VMEM((count, stencil, width, width), BF16),
            pltpu.SemaphoreType.DMA((count,)),
        ],
        compiler_params=params(),
    )(plan, pltpu.with_memory_space_constraint(blocks, pltpu.HBM), before, own, after, *waited)


def pick_kernel(index_ref, first_ref, own_ref, second_ref, mine_ref, waited_ref, out_ref, turned_ref):
    stencil, count = index_ref.shape
    quarter = LANES // 4
    narrow = LANES // 2

    def body(q, carry):
        for k in range(stencil):
            code = index_ref[k, q]
            row = lax.shift_right_logical(code, 2)
            step = code & 3
            out_ref[q * stencil + k] = jnp.where(
                step == 0, first_ref[row], jnp.where(step == 1, own_ref[row], second_ref[row])
            )
        return carry

    lax.fori_loop(0, count, body, 0, unroll=4)
    row = lax.broadcasted_iota(I32, (quarter, LANES), 0)
    lane = lax.broadcasted_iota(I32, (quarter, LANES), 1)
    pick = jnp.where(lane == row % 8 * 4 + row // 8, 1.0, 0.0).astype(BF16)
    old = lax.broadcasted_iota(I32, (narrow, narrow), 0)
    new = lax.broadcasted_iota(I32, (narrow, narrow), 1)
    order = jnp.where(old == new % quarter * 2 + new // quarter, 1.0, 0.0).astype(BF16)

    def turn(q, carry):
        packed = mine_ref[q]
        column = jnp.concatenate([packed] + [pltpu.roll(packed, LANES - h * quarter, 1) for h in range(1, 4)], axis=0)
        turned = lax.dot_general(pick, column, (((1,), (1,)), ((), ())), preferred_element_type=F32)
        turned_ref[q] = jnp.dot(turned.astype(BF16), order, preferred_element_type=F32).astype(BF16)
        return carry

    lax.fori_loop(0, count, turn, 0, unroll=4)


def pick_rows(index, first, own, second, mine, waited):
    stencil, count = index.shape
    return pl.pallas_call(
        pick_kernel,
        out_shape=(
            jax.ShapeDtypeStruct((count * stencil,) + own.shape[1:], own.dtype),
            jax.ShapeDtypeStruct((count, LANES // 4, LANES // 2), own.dtype),
        ),
        in_specs=[smem(), vmem(), vmem(), vmem(), vmem(), hbm()],
        out_specs=(vmem(), vmem()),
        compiler_params=params(),
    )(index, first, own, second, mine, waited)


def owner_kernel(
    where_ref,
    target_ref,
    plan_ref,
    picked_ref,
    own_ref,
    *rest,
    parts,
    capacity,
    capacity2,
    owned,
    stencil,
):
    arrived = rest[:parts]
    out_ref = rest[parts]
    sends = rest[parts + 1 : 2 * parts + 1]
    sum_ref, term_ref = rest[2 * parts + 1 :]
    dom = where_ref[1]
    second_slot = parts * capacity * (stencil + 1)
    flat = sum_ref.shape[1]
    narrow = LANES // 2
    sum_ref[...] = jnp.zeros(sum_ref.shape, F32)
    for d in range(parts):
        part_ref = arrived[d]

        def add(r, carry, d=d, part_ref=part_ref):
            base = (dom * capacity + r) * stencil
            for k in range(stencil):
                target = target_ref[dom ^ d, base + k]
                sum_ref[target] += part_ref[pl.ds((r * stencil + k) * flat, flat), :].astype(F32)
            return carry

        lax.fori_loop(0, capacity, add, 0, unroll=True)

    left = low_lanes((flat, LANES), narrow)
    quarter = LANES // 4
    eighth = lax.broadcasted_iota(I32, (8, LANES), 1) // quarter
    block = lax.broadcasted_iota(I32, (16, LANES), 1) // quarter
    none = jnp.zeros((16, LANES), BF16)

    batch = 2

    def second(step, carry):
        places = [(step * batch + n, r) for n in range(batch) for r in range(capacity2)]
        names = [plan_ref[second_slot + d * capacity2 + r] for d, r in places]
        products = []
        for q in names:
            rows = []
            weights = []
            for k in range(0, stencil, 2):
                one = sum_ref[k * owned + q].astype(BF16)
                out_ref[k * owned + q] = one
                if k + 1 < stencil:
                    two = sum_ref[(k + 1) * owned + q].astype(BF16)
                    out_ref[(k + 1) * owned + q] = two
                else:
                    two = jnp.zeros((flat, LANES), BF16)
                even = jnp.where(left, one, pltpu.roll(two, narrow, 1))
                odd = jnp.where(left, pltpu.roll(one, narrow, 1), two)
                rows.append(jnp.concatenate([even, odd], axis=0))
            for k in range(stencil):
                packed = picked_ref[q * stencil + k]
                for h in range(4):
                    shift = (k - h) % 4 * quarter
                    turned = pltpu.roll(packed, shift, 1) if shift else packed
                    weights.append(jnp.where(block == k % 4, turned, none))
            groups = []
            for g in range((stencil + 3) // 4):
                lhs = jnp.concatenate(rows[2 * g : 2 * g + 2], axis=1)
                rhs = jnp.concatenate(weights[16 * g : 16 * g + 16], axis=0)
                product = jnp.dot(lhs[:, : rhs.shape[0]], rhs, preferred_element_type=F32)
                groups.append(product.astype(BF16))
            products.append(jnp.concatenate(groups, axis=1))
        terms = [jnp.dot(own_ref[q], p, preferred_element_type=F32) for q, p in zip(names, products)]
        for (d, r), term in zip(places, terms):
            for k in range(stencil):
                g = k // 4
                total = None
                for w in range(4):
                    piece = term[w * 8 : (w + 1) * 8, g * LANES : (g + 1) * LANES]
                    shift = (w - k) % 4 * quarter
                    if shift:
                        piece = pltpu.roll(piece, shift, 1)
                    total = piece if total is None else jnp.where(eighth == w, piece, total)
                term_ref[d, pl.ds((r * stencil + k) * 8, 8), :] = total
        return carry

    lax.fori_loop(0, parts // batch, second, 0)
    for d in range(parts):
        sends[d][...] = term_ref[d].astype(BF16)


def owner_level(where, targets, plan, picked, own, arrived, parts, capacity, capacity2, owned, stencil):
    flat = LANES // 4
    send = jax.ShapeDtypeStruct((capacity2 * stencil * 8, LANES), BF16)
    return pl.pallas_call(
        functools.partial(
            owner_kernel, parts=parts, capacity=capacity, capacity2=capacity2, owned=owned, stencil=stencil
        ),
        out_shape=(jax.ShapeDtypeStruct((stencil * owned, flat, LANES), BF16),) + (send,) * parts,
        in_specs=[smem(), smem(), smem()] + [vmem()] * (2 + parts),
        out_specs=(vmem(),) * (1 + parts),
        scratch_shapes=[
            pltpu.VMEM((stencil * owned + 1, flat, LANES), F32),
            pltpu.VMEM((parts, capacity2 * stencil * 8, LANES), F32),
        ],
        compiler_params=params(),
    )(where, targets, plan, picked, own, *arrived)


def final_kernel(where_ref, target_ref, *rest, parts, first, capacity2, stencil):
    arrived = rest[:parts]
    out_ref = rest[parts]
    (sum_ref,) = rest[parts + 1 :]
    dom = where_ref[1]
    deep = stencil + 1
    sum_ref[...] = jnp.zeros(sum_ref.shape, F32)
    for d in range(parts):
        values = arrived[d][...].astype(F32)
        for r in range(capacity2):
            base = (first + dom * capacity2 + r) * stencil
            for k in range(stencil):
                at = r * stencil + k
                sum_ref[target_ref[dom ^ d, base + k]] += values[at * 8 : (at + 1) * 8]
    for u in range(out_ref.shape[0]):
        for t in range(8):
            tile = sum_ref[pl.ds(u * deep, deep), t, :]
            out_ref[u, :, pl.ds(t * LANES, LANES)] = tile[:stencil].astype(BF16)


def final_level(where, targets, arrived, parts, first, capacity2, owned2, stencil):
    return pl.pallas_call(
        functools.partial(final_kernel, parts=parts, first=first, capacity2=capacity2, stencil=stencil),
        out_shape=jax.ShapeDtypeStruct((owned2, stencil, 8 * LANES), BF16),
        in_specs=[smem(), smem()] + [vmem()] * parts,
        out_specs=vmem(),
        scratch_shapes=[pltpu.VMEM((owned2 * (stencil + 1) + 1, 8, LANES), F32)],
        compiler_params=params(),
    )(where, targets, *arrived)


def chunks_of(parts):
    order = sorted(range(parts), key=lambda d: (-(d >> 1).bit_count(), -(d & 1), -d))
    return [tuple(order[i : i + 2]) for i in range(0, parts, 2)]


def local(
    fine_blocks,
    interp,
    fine_cols,
    fine_slot,
    fine_owner,
    fine_place,
    coarse_interp,
    coarse_cols,
    coarse_slot,
    coarse_owner,
    coarse_place,
):
    rows, stencil, width, _ = fine_blocks.shape
    narrow = interp.shape[1] // width
    parts = lax.axis_size("dom")
    region = lax.axis_index("region")
    dom = lax.axis_index("dom")
    owned = rows // 2
    owned2 = owned // 2
    capacity = max(2, rows // 8)
    capacity2 = max(2, owned // 8)
    slots = parts * capacity
    slots2 = parts * capacity2
    where = jnp.stack([region, dom]).astype(I32)

    own = halves(interp)
    halo = neighbours(own, "region")

    plan, target, quarters = pl.pallas_call(
        functools.partial(
            index_kernel, parts=parts, capacity=capacity, capacity2=capacity2, owned=owned, owned2=owned2
        ),
        out_shape=(
            jax.ShapeDtypeStruct((slots * (stencil + 1) + slots2,), I32),
            jax.ShapeDtypeStruct(((slots + slots2) * stencil,), I32),
            jax.ShapeDtypeStruct((owned, coarse_interp.shape[1] // LANES, LANES), BF16),
        ),
        in_specs=[smem()] * 8 + [vmem()],
        out_specs=(smem(), smem(), vmem()),
        scratch_shapes=[pltpu.SMEM((parts,), I32), pltpu.VMEM((coarse_interp.size // LANES, LANES), F32)],
        compiler_params=params(),
    )(
        where,
        fine_cols.T,
        fine_slot.T,
        fine_owner[:, 0],
        fine_place,
        coarse_slot.T,
        coarse_owner[:, 0],
        lax.optimization_barrier((coarse_place, own))[0],
        coarse_interp,
    )

    size2 = coarse_interp.shape[1]
    extra = pl.cdiv(target.shape[0], size2)
    codes = jnp.pad(target, (0, extra * size2 - target.shape[0])).astype(BF16)
    stacked = jnp.concatenate([quarters, codes.reshape((extra,) + quarters.shape[1:])], axis=0)
    table = lax.all_gather(stacked, "dom", axis=0, tiled=True)
    pitch = owned + extra
    targets = table.reshape((parts, pitch) + quarters.shape[1:])[:, owned:].reshape(parts, extra * size2)
    targets = targets[:, : target.shape[0]].astype(I32)

    tables = neighbours(table, "region")
    arrived = [None] * parts
    chunks = chunks_of(parts)
    sent = ()
    for n, offsets in enumerate(chunks):
        waited = tuple(sent[:1])
        if n == 2:
            waited = waited + tables
        if n >= 3:
            waited = waited + (arrived[chunks[n - 3][0]],)
        sent = level_one(plan, fine_blocks, halo[0], own, halo[1], offsets, capacity, slots, waited)
        for offset, cells in zip(offsets, sent):
            arrived[offset] = exchange(cells, "dom", offset) if offset else cells
    span2 = parts * owned
    inside = coarse_cols % span2
    step2 = table_of(coarse_cols // span2 - region + 1, region)
    index2 = (inside // owned * pitch + inside % owned) * 4 + step2
    picked, turned = pick_rows(index2.T, tables[0], table, tables[1], quarters, sent[0])
    outs = owner_level(
        where, targets, plan, picked, turned, arrived, parts, capacity, capacity2, owned, stencil
    )
    coarse_blocks = outs[0].reshape(stencil, owned, narrow * narrow).transpose(1, 0, 2)
    arrived2 = list(outs[1:])
    for d in range(parts - 1, 0, -1):
        arrived2[d] = exchange(arrived2[d], "dom", d)
    second = final_level(where, targets, arrived2, parts, slots, capacity2, owned2, stencil)
    return (coarse_blocks, second)


def solution(mesh):
    in_specs = (
        P(("region", "dom"), None, None, None),
        P(("region", "dom"), None),
        P(("region", "dom"), None),
        P(("region", "dom"), None),
        P(("region", "dom"), None),
        P(("region", "dom")),
        P(("region", "dom"), None),
        P(("region", "dom"), None),
        P(("region", "dom"), None),
        P(("region", "dom"), None),
        P(("region", "dom")),
    )
    out_specs = (P(("region", "dom"), None, None), P(("region", "dom"), None, None))
    return jax.shard_map(local, mesh=mesh, in_specs=in_specs, out_specs=out_specs, check_vma=False)
```

```python
import functools

import jax
import jax.numpy as jnp
from jax import lax
from jax.experimental import pallas as pl
from jax.experimental.pallas import tpu as pltpu
from jax.sharding import PartitionSpec as P

BF16 = jnp.bfloat16
F32 = jnp.float32
I32 = jnp.int32
LANES = 128
VMEM_LIMIT = 32 * 1024 * 1024


def vmem():
    return pl.BlockSpec(memory_space=pltpu.VMEM)


def smem():
    return pl.BlockSpec(memory_space=pltpu.SMEM)


def hbm():
    return pl.BlockSpec(memory_space=pl.ANY)


def params():
    return pltpu.CompilerParams(vmem_limit_bytes=VMEM_LIMIT)


def low_lanes(shape, bound):
    return lax.broadcasted_iota(I32, shape, len(shape) - 1) < bound


def exchange(cells, axis, offset):
    count = lax.axis_size(axis)
    return lax.ppermute(cells, axis, [(i, i ^ offset) for i in range(count)])


def partner(index, odd, count):
    other = ((index + odd) ^ 1) - odd
    return other if 0 <= other < count else index


def neighbours(cells, axis):
    count = lax.axis_size(axis)
    return tuple(lax.ppermute(cells, axis, [(i, partner(i, odd, count)) for i in range(count)]) for odd in (0, 1))


def table_of(step, region):
    swapped = jnp.where(region % 2 == 0, 2 - step, step)
    return jnp.where(step == 1, 1, swapped)


def halves_kernel(flat_ref, out_ref, rows_ref, wide_ref, sems):
    steps, group = rows_ref.shape[:2]
    deep = rows_ref.shape[2] // LANES
    half = deep // 2
    left = low_lanes((group, LANES), LANES // 2)

    def copy(g):
        return pltpu.make_async_copy(flat_ref.at[pl.ds(g * group, group)], rows_ref.at[g], sems.at[g])

    for g in range(steps):
        copy(g).start()
    for g in range(steps):
        copy(g).wait()
        for t in range(half):
            upper = rows_ref[g, :, pl.ds(t * LANES, LANES)].astype(F32)
            lower = rows_ref[g, :, pl.ds((t + half) * LANES, LANES)].astype(F32)
            even = jnp.where(left, upper, pltpu.roll(lower, LANES // 2, 1))
            odd = jnp.where(left, pltpu.roll(upper, LANES // 2, 1), lower)
            wide_ref[g, pl.ds(2 * t, group, stride=deep), :] = even
            wide_ref[g, pl.ds(2 * t + 1, group, stride=deep), :] = odd
        for r in range(group):
            out_ref[g * group + r] = wide_ref[g, pl.ds(r * deep, deep), :].astype(BF16)


def halves(flat):
    rows, size = flat.shape
    deep = size // LANES
    group = 16
    steps = rows // group
    return pl.pallas_call(
        halves_kernel,
        out_shape=jax.ShapeDtypeStruct((rows, deep, LANES), BF16),
        in_specs=[pl.BlockSpec(memory_space=pltpu.HBM)],
        out_specs=vmem(),
        scratch_shapes=[
            pltpu.VMEM((steps, group, size), BF16),
            pltpu.VMEM((steps, group * deep, LANES), F32),
            pltpu.SemaphoreType.DMA((steps,)),
        ],
        compiler_params=params(),
    )(pltpu.with_memory_space_constraint(flat, pltpu.HBM))


def quarters_of(coarse_ref, quarters_ref, wide_ref):
    count = coarse_ref.shape[0]
    deep = coarse_ref.shape[1] // LANES
    quarter = LANES // 4
    lane = lax.broadcasted_iota(I32, (count, LANES), 1) // quarter
    for t in range(deep // 4):
        tiles = [coarse_ref[:, pl.ds((h * deep // 4 + t) * LANES, LANES)].astype(F32) for h in range(4)]
        for u in range(4):
            total = None
            for h in range(4):
                shift = (h - u) % 4 * quarter
                piece = pltpu.roll(tiles[h], shift, 1) if shift else tiles[h]
                total = piece if total is None else jnp.where(lane == h, piece, total)
            wide_ref[pl.ds(4 * t + u, count, stride=deep), :] = total
    for r in range(count):
        quarters_ref[r] = wide_ref[pl.ds(r * deep, deep), :].astype(BF16)


def owner_order(owner_ref, wide_ref, capacity):
    count = owner_ref.shape[1]
    square = (LANES, LANES)
    down = lax.broadcasted_iota(I32, square, 0).astype(F32)
    along = lax.broadcasted_iota(I32, square, 1).astype(F32)
    wide_ref[...] = jnp.full(wide_ref.shape, -1.0, F32)
    wide_ref[0:1, 0:count] = owner_ref[...].astype(F32)
    owner = wide_ref[0:1, :]
    across = jnp.broadcast_to(owner, square)
    earlier = jnp.where((across == across.T) & (down < along), 1.0, 0.0)
    rank = jnp.sum(earlier, axis=0, keepdims=True)
    position = jnp.where(owner >= 0.0, owner * capacity + rank, -1.0)
    named = jnp.broadcast_to(position, square).T == along
    hit = jnp.sum(jnp.where(named, 1.0, 0.0), axis=0, keepdims=True)
    row = jnp.sum(jnp.where(named, down, 0.0), axis=0, keepdims=True)
    return (row + (1.0 - hit) * count).astype(I32)


def index_kernel(where_ref, *rest, **sizes):
    inputs = rest[:8]
    info_ref, stacked_ref, wide_ref, narrow_ref = rest[9:13]
    locals_ = rest[13:21]
    sems = rest[21]
    copies = [pltpu.make_async_copy(a, b, sems.at[n]) for n, (a, b) in enumerate(zip(inputs, locals_))]
    for copy in copies:
        copy.start()
    for copy in copies:
        copy.wait()
    fill_tables(where_ref, *locals_, info_ref, stacked_ref, wide_ref, narrow_ref, **sizes)


def fill_tables(
    where_ref,
    cols_ref,
    slot_ref,
    owner_ref,
    place_ref,
    slot2_ref,
    owner2_ref,
    place2_ref,
    coarse_ref,
    info_ref,
    stacked_ref,
    wide_ref,
    narrow_ref,
    *,
    parts,
    capacity,
    capacity2,
    owned,
    owned2,
):
    region = where_ref[0]
    dom = where_ref[1]
    stencil, rows = cols_ref.shape
    rows2 = slot2_ref.shape[1]
    group = stencil + 1
    span = parts * rows
    first = region * span
    quarters_of(coarse_ref, stacked_ref, wide_ref)
    info_ref[0:group, :] = jnp.full((group, LANES), stencil * owned, I32)
    info_ref[group : 2 * group, :] = jnp.full((group, LANES), group * owned2, I32)
    info_ref[2 * group :, :] = jnp.full((group, LANES), dom, I32)
    info_ref[0:stencil, 0:rows] = slot_ref[...] * owned + place_ref[...]
    info_ref[group : group + stencil, 0:rows2] = place2_ref[...] * group + slot2_ref[...]
    cols = cols_ref[...]
    step = jnp.where(cols < first, 0, jnp.where(cols >= first + span, 2, 1))
    begin = ((region + step - 1) * parts + dom) * rows
    info_ref[2 * group : 2 * group + stencil, 0:rows] = (cols - begin) * 4 + table_of(step, region)
    info_ref[stencil : stencil + 1, :] = owner_order(owner_ref, narrow_ref, capacity)
    info_ref[group + stencil : 2 * group, :] = owner_order(owner2_ref, narrow_ref, capacity2)
    stacked_ref[rows2] = info_ref[0 : 2 * group, :].astype(F32).astype(BF16)


def terms_kernel(table_ref, blocks_ref, before_ref, own_ref, after_ref, *rest, offsets, capacity, waited):
    outs = rest[waited : waited + len(offsets)]
    info_ref, buffer_ref, info_sem, row_sem = rest[waited + len(offsets) :]
    stencil, width = buffer_ref.shape[1], buffer_ref.shape[2]
    half = width // 2
    narrow = LANES // 2
    flat = narrow * narrow // LANES

    table_copy = pltpu.make_async_copy(table_ref, info_ref, info_sem)
    table_copy.start()
    table_copy.wait()
    dom = info_ref[3 * (stencil + 1) - 1, 0]

    def source_of(offset, r):
        return jnp.minimum(info_ref[stencil, (dom ^ offset) * capacity + r], own_ref.shape[0] - 1)

    def row_copy(n, source):
        return pltpu.make_async_copy(blocks_ref.at[source], buffer_ref.at[n], row_sem.at[n])

    for n, offset in enumerate(offsets):
        for r in range(capacity):
            row_copy(n * capacity + r, source_of(offset, r)).start()

    left = low_lanes((half, LANES), narrow)
    left_flat = low_lanes((flat, LANES), narrow)
    out_row = lax.broadcasted_iota(I32, (narrow, LANES), 0)
    in_col = lax.broadcasted_iota(I32, (narrow, LANES), 1)
    chosen = jnp.where(out_row < flat, 2 * out_row, 2 * (out_row - flat) + 1)
    pick = jnp.where(in_col == chosen, 1.0, 0.0).astype(BF16)
    zero = jnp.zeros((half, LANES), BF16)

    def neighbour(source, k):
        code = info_ref[2 * (stencil + 1) + k, source]
        row = lax.shift_right_logical(code, 2)
        step = code & 3
        return jnp.where(step == 0, before_ref[row], jnp.where(step == 1, own_ref[row], after_ref[row]))

    def one_row(n, source, out_ref, r):
        mine = own_ref[source]
        column = jnp.concatenate([mine, pltpu.roll(mine, narrow, 1)], axis=0)
        turned = lax.dot_general(
            pick, column, (((1,), (1,)), ((), ())), preferred_element_type=F32
        ).astype(BF16)
        products = []
        for k in range(0, stencil, 2):
            one = neighbour(source, k)
            weights = [jnp.where(left, one, zero), jnp.where(left, pltpu.roll(one, narrow, 1), zero)]
            lhs = buffer_ref[n, k]
            if k + 1 < stencil:
                two = neighbour(source, k + 1)
                weights += [jnp.where(left, zero, pltpu.roll(two, narrow, 1)), jnp.where(left, zero, two)]
                lhs = jnp.concatenate([lhs, buffer_ref[n, k + 1]], axis=1)
            products.append(
                jnp.dot(lhs, jnp.concatenate(weights, axis=0), preferred_element_type=F32).astype(BF16)
            )
        term = jnp.dot(turned, jnp.concatenate(products, axis=1), preferred_element_type=F32)
        for k in range(0, stencil, 2):
            pair = term[:, k // 2 * LANES : (k // 2 + 1) * LANES]
            even = pair[:flat]
            odd = pair[flat:]
            base = (r * stencil + k) * flat
            out_ref[pl.ds(base, flat), :] = jnp.where(left_flat, even, pltpu.roll(odd, narrow, 1)).astype(BF16)
            if k + 1 < stencil:
                out_ref[pl.ds(base + flat, flat), :] = jnp.where(
                    left_flat, pltpu.roll(even, narrow, 1), odd
                ).astype(BF16)

    for n, offset in enumerate(offsets):
        sources = [source_of(offset, r) for r in range(capacity)]
        for r, source in enumerate(sources):
            row_copy(n * capacity + r, source).wait()
        for r, source in enumerate(sources):
            one_row(n * capacity + r, source, outs[n], r)


def level_one(info, blocks, before, own, after, offsets, capacity, waited):
    rows, stencil, width, _ = blocks.shape
    narrow = LANES // 2
    flat = narrow * narrow // LANES
    shape = jax.ShapeDtypeStruct((capacity * stencil * flat, LANES), BF16)
    count = len(offsets) * capacity
    return pl.pallas_call(
        functools.partial(terms_kernel, offsets=offsets, capacity=capacity, waited=len(waited)),
        out_shape=tuple(shape for _ in offsets),
        in_specs=[hbm(), hbm(), vmem(), vmem(), vmem()] + [hbm()] * len(waited),
        out_specs=tuple(vmem() for _ in offsets),
        scratch_shapes=[
            pltpu.SMEM(info.shape, I32),
            pltpu.VMEM((count, stencil, width, width), BF16),
            pltpu.SemaphoreType.DMA(()),
            pltpu.SemaphoreType.DMA((count,)),
        ],
        compiler_params=params(),
    )(
        pltpu.with_memory_space_constraint(info, pltpu.HBM),
        pltpu.with_memory_space_constraint(blocks, pltpu.HBM),
        before,
        own,
        after,
        *waited,
    )


def pick_kernel(index_ref, first_ref, own_ref, second_ref, mine_ref, waited_ref, out_ref, turned_ref):
    stencil, count = index_ref.shape
    quarter = LANES // 4
    narrow = LANES // 2

    def body(q, carry):
        for k in range(stencil):
            code = index_ref[k, q]
            row = lax.shift_right_logical(code, 2)
            step = code & 3
            out_ref[q * stencil + k] = jnp.where(
                step == 0, first_ref[row], jnp.where(step == 1, own_ref[row], second_ref[row])
            )
        return carry

    lax.fori_loop(0, count, body, 0, unroll=4)
    square = (LANES, LANES)
    row = lax.broadcasted_iota(I32, square, 0)
    lane = lax.broadcasted_iota(I32, square, 1)
    old = row // quarter * quarter + row % 8 * 4 + row % quarter // 8
    pick = jnp.where(lane == old, 1.0, 0.0).astype(BF16)
    new = lax.broadcasted_iota(I32, (narrow, narrow), 0)
    old = lax.broadcasted_iota(I32, (narrow, narrow), 1)
    order = jnp.where(old == new % quarter * 2 + new // quarter, 1.0, 0.0).astype(BF16)
    block = lax.broadcasted_iota(I32, (16, LANES), 1) // quarter
    columns = []
    for g in range(count // 4):
        pieces = []
        for h in range(4):
            total = None
            for n in range(4):
                shift = (n - h) % 4 * quarter
                piece = mine_ref[4 * g + n]
                piece = pltpu.roll(piece, shift, 1) if shift else piece
                total = piece if total is None else jnp.where(block == n, piece, total)
            pieces.append(total)
        columns.append(jnp.concatenate(pieces, axis=0))
    ordered = [jnp.dot(order, column, preferred_element_type=F32).astype(BF16) for column in columns]
    for g, column in enumerate(ordered):
        turned = lax.dot_general(pick, column, (((1,), (1,)), ((), ())), preferred_element_type=F32).astype(BF16)
        for n in range(4):
            turned_ref[4 * g + n] = turned[n * quarter : (n + 1) * quarter]


def pick_rows(index, first, own, second, mine, waited):
    stencil, count = index.shape
    return pl.pallas_call(
        pick_kernel,
        out_shape=(
            jax.ShapeDtypeStruct((count * stencil,) + own.shape[1:], own.dtype),
            jax.ShapeDtypeStruct((count, LANES // 4, LANES // 2), own.dtype),
        ),
        in_specs=[smem(), vmem(), vmem(), vmem(), vmem(), hbm()],
        out_specs=(vmem(), vmem()),
        compiler_params=params(),
    )(index, first, own, second, mine, waited)


def add_terms(dom, target_ref, arrived, offsets, sum_ref, capacity, stencil):
    flat = sum_ref.shape[1]
    for d, part_ref in zip(offsets, arrived):
        base = (dom ^ d) * 2 * (stencil + 1)
        for r in range(capacity):
            row = target_ref[base + stencil, dom * capacity + r]
            for k in range(stencil):
                target = target_ref[base + k, row]
                sum_ref[target] += part_ref[pl.ds((r * stencil + k) * flat, flat), :].astype(F32)


def early_kernel(where_ref, target_ref, *rest, offsets, capacity, stencil):
    sum_ref = rest[-1]
    sum_ref[...] = jnp.zeros(sum_ref.shape, F32)
    add_terms(where_ref[1], target_ref, rest[: len(offsets)], offsets, sum_ref, capacity, stencil)


def early_sums(where, targets, waited, arrived, offsets, capacity, owned, stencil):
    return pl.pallas_call(
        functools.partial(early_kernel, offsets=offsets, capacity=capacity, stencil=stencil),
        out_shape=jax.ShapeDtypeStruct((stencil * owned + 1, LANES // 4, LANES), F32),
        in_specs=[smem(), smem()] + [vmem()] * len(offsets) + [hbm()],
        out_specs=vmem(),
        compiler_params=params(),
    )(where, targets, *arrived, waited)


def owner_kernel(
    where_ref,
    target_ref,
    picked_ref,
    own_ref,
    early_ref,
    *rest,
    parts,
    offsets,
    capacity,
    capacity2,
    owned,
    stencil,
):
    arrived = rest[: len(offsets)]
    out_ref = rest[len(offsets)]
    sum_ref = rest[len(offsets) + 1]
    sends = rest[len(offsets) + 2 : len(offsets) + 2 + parts]
    (term_ref,) = rest[len(offsets) + 2 + parts :]
    dom = where_ref[1]
    group = stencil + 1
    mine = dom * 2 * group
    flat = sum_ref.shape[1]
    narrow = LANES // 2
    add_terms(dom, target_ref, arrived, offsets, sum_ref, capacity, stencil)

    left = low_lanes((flat, LANES), narrow)
    quarter = LANES // 4
    eighth = lax.broadcasted_iota(I32, (8, LANES), 1) // quarter
    block = lax.broadcasted_iota(I32, (16, LANES), 1) // quarter
    none = jnp.zeros((16, LANES), BF16)

    batch = 2

    def second(step, carry):
        places = [(step * batch + n, r) for n in range(batch) for r in range(capacity2)]
        names = [
            jnp.minimum(target_ref[mine + 2 * group - 1, (dom ^ d) * capacity2 + r], owned - 1) for d, r in places
        ]
        products = []
        for q in names:
            rows = []
            weights = []
            for k in range(0, stencil, 2):
                one = sum_ref[k * owned + q].astype(BF16)
                out_ref[k * owned + q] = one
                if k + 1 < stencil:
                    two = sum_ref[(k + 1) * owned + q].astype(BF16)
                    out_ref[(k + 1) * owned + q] = two
                else:
                    two = jnp.zeros((flat, LANES), BF16)
                even = jnp.where(left, one, pltpu.roll(two, narrow, 1))
                odd = jnp.where(left, pltpu.roll(one, narrow, 1), two)
                rows.append(jnp.concatenate([even, odd], axis=0))
            for k in range(stencil):
                packed = picked_ref[q * stencil + k]
                for h in range(4):
                    shift = (k - h) % 4 * quarter
                    turned = pltpu.roll(packed, shift, 1) if shift else packed
                    weights.append(jnp.where(block == k % 4, turned, none))
            groups = []
            for g in range((stencil + 3) // 4):
                lhs = jnp.concatenate(rows[2 * g : 2 * g + 2], axis=1)
                rhs = jnp.concatenate(weights[16 * g : 16 * g + 16], axis=0)
                product = jnp.dot(lhs[:, : rhs.shape[0]], rhs, preferred_element_type=F32)
                groups.append(product.astype(BF16))
            products.append(jnp.concatenate(groups, axis=1))
        terms = [jnp.dot(own_ref[q], p, preferred_element_type=F32) for q, p in zip(names, products)]
        for (d, r), term in zip(places, terms):
            for k in range(stencil):
                g = k // 4
                total = None
                for w in range(4):
                    piece = term[w * 8 : (w + 1) * 8, g * LANES : (g + 1) * LANES]
                    shift = (w - k) % 4 * quarter
                    if shift:
                        piece = pltpu.roll(piece, shift, 1)
                    total = piece if total is None else jnp.where(eighth == w, piece, total)
                term_ref[d, pl.ds((r * stencil + k) * 8, 8), :] = total
        return carry

    lax.fori_loop(0, parts // batch, second, 0)
    for d in range(parts):
        sends[d][...] = term_ref[d].astype(BF16)


def owner_level(where, targets, picked, own, early, arrived, offsets, parts, capacity, capacity2, owned, stencil):
    flat = LANES // 4
    send = jax.ShapeDtypeStruct((capacity2 * stencil * 8, LANES), BF16)
    return pl.pallas_call(
        functools.partial(
            owner_kernel,
            parts=parts,
            offsets=offsets,
            capacity=capacity,
            capacity2=capacity2,
            owned=owned,
            stencil=stencil,
        ),
        out_shape=(
            jax.ShapeDtypeStruct((stencil * owned, flat, LANES), BF16),
            jax.ShapeDtypeStruct(early.shape, F32),
        )
        + (send,) * parts,
        in_specs=[smem(), smem()] + [vmem()] * (3 + len(offsets)),
        out_specs=(vmem(),) * (2 + parts),
        scratch_shapes=[pltpu.VMEM((parts, capacity2 * stencil * 8, LANES), F32)],
        input_output_aliases={4: 1},
        compiler_params=params(),
    )(where, targets, picked, own, early, *arrived)


def final_kernel(where_ref, target_ref, *rest, parts, capacity2, stencil):
    arrived = rest[:parts][::-1]
    out_ref = rest[parts]
    sum_ref, other_ref = rest[parts + 1 :]
    dom = where_ref[1]
    deep = stencil + 1
    other_ref[...] = jnp.zeros(other_ref.shape, F32)
    sum_ref[...] = jnp.zeros(sum_ref.shape, F32)
    for d in range(0, parts, 2):
        pairs = [(sum_ref, d), (other_ref, d + 1)]
        values = [arrived[e][...].astype(F32) for _, e in pairs]
        for r in range(capacity2):
            bases = [((dom ^ e) * 2 + 1) * deep for _, e in pairs]
            rows = [target_ref[base + stencil, dom * capacity2 + r] for base in bases]
            for k in range(stencil):
                at = r * stencil + k
                for (into_ref, _), base, row, value in zip(pairs, bases, rows, values):
                    into_ref[target_ref[base + k, row]] += value[at * 8 : (at + 1) * 8]
    for u in range(out_ref.shape[0]):
        for t in range(8):
            tile = sum_ref[pl.ds(u * deep, deep), t, :] + other_ref[pl.ds(u * deep, deep), t, :]
            out_ref[u, :, pl.ds(t * LANES, LANES)] = tile[:stencil].astype(BF16)


def final_level(where, targets, arrived, parts, capacity2, owned2, stencil):
    return pl.pallas_call(
        functools.partial(final_kernel, parts=parts, capacity2=capacity2, stencil=stencil),
        out_shape=jax.ShapeDtypeStruct((owned2, stencil, 8 * LANES), BF16),
        in_specs=[smem(), smem()] + [vmem()] * parts,
        out_specs=vmem(),
        scratch_shapes=[pltpu.VMEM((owned2 * (stencil + 1) + 1, 8, LANES), F32)] * 2,
        compiler_params=params(),
    )(where, targets, *arrived[::-1])


def chunks_of(parts):
    order = sorted(range(parts), key=lambda d: (-(d >> 1).bit_count(), -(d & 1), -d))
    return [tuple(order[i : i + 2]) for i in range(0, parts, 2)]


def local(
    fine_blocks,
    interp,
    fine_cols,
    fine_slot,
    fine_owner,
    fine_place,
    coarse_interp,
    coarse_cols,
    coarse_slot,
    coarse_owner,
    coarse_place,
):
    rows, stencil, width, _ = fine_blocks.shape
    narrow = interp.shape[1] // width
    parts = lax.axis_size("dom")
    region = lax.axis_index("region")
    dom = lax.axis_index("dom")
    owned = rows // 2
    owned2 = owned // 2
    capacity = max(2, rows // 8)
    capacity2 = max(2, owned // 8)
    where = jnp.stack([region, dom]).astype(I32)

    own = halves(interp)
    halo = neighbours(own, "region")

    size2 = coarse_interp.shape[1]
    group = stencil + 1
    inputs = [
        fine_cols.T,
        fine_slot.T,
        fine_owner.T,
        fine_place.reshape(1, rows),
        coarse_slot.T,
        coarse_owner.T,
        coarse_place.reshape(1, owned),
        coarse_interp,
    ]
    info, stacked = pl.pallas_call(
        functools.partial(
            index_kernel, parts=parts, capacity=capacity, capacity2=capacity2, owned=owned, owned2=owned2
        ),
        out_shape=(
            jax.ShapeDtypeStruct((3 * group, LANES), I32),
            jax.ShapeDtypeStruct((owned + 1, size2 // LANES, LANES), BF16),
        ),
        in_specs=[smem()] + [hbm()] * 9,
        out_specs=(vmem(), vmem()),
        scratch_shapes=[pltpu.VMEM((coarse_interp.size // LANES, LANES), F32), pltpu.VMEM((8, LANES), F32)]
        + [pltpu.VMEM(x.shape, x.dtype) for x in inputs]
        + [pltpu.SemaphoreType.DMA((len(inputs),))],
        compiler_params=params(),
    )(where, *[pltpu.with_memory_space_constraint(x, pltpu.HBM) for x in inputs], own)

    table = lax.all_gather(stacked, "dom", axis=0, tiled=True)
    pitch = owned + 1
    targets = table.reshape((parts, pitch, 2 * group, LANES))[:, owned].reshape(parts * 2 * group, LANES).astype(I32)

    tables = neighbours(table, "region")
    arrived = [None] * parts
    chunks = chunks_of(parts)
    sent = ()
    for n, offsets in enumerate(chunks):
        waited = tuple(sent[:1])
        if n == 2:
            waited = waited + tables
        if n >= 3:
            waited = waited + tuple(arrived[d] for d in chunks[n - 3])
        sent = level_one(info, fine_blocks, halo[0], own, halo[1], offsets, capacity, waited)
        for offset, cells in zip(offsets, sent):
            arrived[offset] = exchange(cells, "dom", offset) if offset else cells
    span2 = parts * owned
    inside = coarse_cols % span2
    step2 = table_of(coarse_cols // span2 - region + 1, region)
    index2 = (inside // owned * pitch + inside % owned) * 4 + step2
    picked, turned = pick_rows(index2.T, tables[0], table, tables[1], stacked, sent[0])
    soon = [0] + [d for offsets in chunks[: len(chunks) // 2] for d in offsets]
    late = [d for d in range(parts) if d not in soon]
    early = early_sums(where, targets, picked, [arrived[d] for d in soon], soon, capacity, owned, stencil)
    outs = owner_level(
        where,
        targets,
        picked,
        turned,
        early,
        [arrived[d] for d in late],
        late,
        parts,
        capacity,
        capacity2,
        owned,
        stencil,
    )
    coarse_blocks = outs[0].reshape(stencil, owned, narrow * narrow).transpose(1, 0, 2)
    arrived2 = list(outs[2:])
    for d in range(parts - 1, 0, -1):
        arrived2[d] = exchange(arrived2[d], "dom", d)
    second = final_level(where, targets, arrived2, parts, capacity2, owned2, stencil)
    return (coarse_blocks, second)


def solution(mesh):
    in_specs = (
        P(("region", "dom"), None, None, None),
        P(("region", "dom"), None),
        P(("region", "dom"), None),
        P(("region", "dom"), None),
        P(("region", "dom"), None),
        P(("region", "dom")),
        P(("region", "dom"), None),
        P(("region", "dom"), None),
        P(("region", "dom"), None),
        P(("region", "dom"), None),
        P(("region", "dom")),
    )
    out_specs = (P(("region", "dom"), None, None), P(("region", "dom"), None, None))
    return jax.shard_map(local, mesh=mesh, in_specs=in_specs, out_specs=out_specs, check_vma=False)
```

```python
import functools

import jax
import jax.numpy as jnp
from jax import lax
from jax.experimental import pallas as pl
from jax.experimental.pallas import tpu as pltpu
from jax.sharding import PartitionSpec as P

BF16 = jnp.bfloat16
F32 = jnp.float32
I32 = jnp.int32
LANES = 128
VMEM_LIMIT = 32 * 1024 * 1024


def vmem():
    return pl.BlockSpec(memory_space=pltpu.VMEM)


def smem():
    return pl.BlockSpec(memory_space=pltpu.SMEM)


def hbm():
    return pl.BlockSpec(memory_space=pl.ANY)


def params():
    return pltpu.CompilerParams(vmem_limit_bytes=VMEM_LIMIT)


def low_lanes(shape, bound):
    return lax.broadcasted_iota(I32, shape, len(shape) - 1) < bound


def exchange(cells, axis, offset):
    count = lax.axis_size(axis)
    return lax.ppermute(cells, axis, [(i, i ^ offset) for i in range(count)])


def partner(index, odd, count):
    other = ((index + odd) ^ 1) - odd
    return other if 0 <= other < count else index


def neighbours(cells, axis):
    count = lax.axis_size(axis)
    return tuple(lax.ppermute(cells, axis, [(i, partner(i, odd, count)) for i in range(count)]) for odd in (1, 0))


def table_of(step, region):
    swapped = jnp.where(region % 2 == 0, step, 2 - step)
    return jnp.where(step == 1, 1, swapped)


def halves_kernel(flat_ref, out_ref, rows_ref, wide_ref, sems):
    steps, group = rows_ref.shape[:2]
    deep = rows_ref.shape[2] // LANES
    half = deep // 2
    left = low_lanes((group, LANES), LANES // 2)

    def copy(g):
        return pltpu.make_async_copy(flat_ref.at[pl.ds(g * group, group)], rows_ref.at[g], sems.at[g])

    for g in range(steps):
        copy(g).start()
    for g in range(steps):
        copy(g).wait()
        for t in range(half):
            upper = rows_ref[g, :, pl.ds(t * LANES, LANES)].astype(F32)
            lower = rows_ref[g, :, pl.ds((t + half) * LANES, LANES)].astype(F32)
            even = jnp.where(left, upper, pltpu.roll(lower, LANES // 2, 1))
            odd = jnp.where(left, pltpu.roll(upper, LANES // 2, 1), lower)
            wide_ref[g, pl.ds(2 * t, group, stride=deep), :] = even
            wide_ref[g, pl.ds(2 * t + 1, group, stride=deep), :] = odd
        for r in range(group):
            out_ref[g * group + r] = wide_ref[g, pl.ds(r * deep, deep), :].astype(BF16)


def halves(flat):
    rows, size = flat.shape
    deep = size // LANES
    group = 16
    steps = rows // group
    return pl.pallas_call(
        halves_kernel,
        out_shape=jax.ShapeDtypeStruct((rows, deep, LANES), BF16),
        in_specs=[pl.BlockSpec(memory_space=pltpu.HBM)],
        out_specs=vmem(),
        scratch_shapes=[
            pltpu.VMEM((steps, group, size), BF16),
            pltpu.VMEM((steps, group * deep, LANES), F32),
            pltpu.SemaphoreType.DMA((steps,)),
        ],
        compiler_params=params(),
    )(pltpu.with_memory_space_constraint(flat, pltpu.HBM))


def quarters_of(coarse_ref, quarters_ref, wide_ref):
    count = coarse_ref.shape[0]
    deep = coarse_ref.shape[1] // LANES
    quarter = LANES // 4
    lane = lax.broadcasted_iota(I32, (count, LANES), 1) // quarter
    for t in range(deep // 4):
        tiles = [coarse_ref[:, pl.ds((h * deep // 4 + t) * LANES, LANES)].astype(F32) for h in range(4)]
        for u in range(4):
            total = None
            for h in range(4):
                shift = (h - u) % 4 * quarter
                piece = pltpu.roll(tiles[h], shift, 1) if shift else tiles[h]
                total = piece if total is None else jnp.where(lane == h, piece, total)
            wide_ref[pl.ds(4 * t + u, count, stride=deep), :] = total
    for r in range(count):
        quarters_ref[r] = wide_ref[pl.ds(r * deep, deep), :].astype(BF16)


def owner_order(owner_ref, wide_ref, capacity):
    count = owner_ref.shape[1]
    square = (LANES, LANES)
    down = lax.broadcasted_iota(I32, square, 0).astype(F32)
    along = lax.broadcasted_iota(I32, square, 1).astype(F32)
    wide_ref[...] = jnp.full(wide_ref.shape, -1.0, F32)
    wide_ref[0:1, 0:count] = owner_ref[...].astype(F32)
    owner = wide_ref[0:1, :]
    across = jnp.broadcast_to(owner, square)
    earlier = jnp.where((across == across.T) & (down < along), 1.0, 0.0)
    rank = jnp.sum(earlier, axis=0, keepdims=True)
    position = jnp.where(owner >= 0.0, owner * capacity + rank, -1.0)
    named = jnp.broadcast_to(position, square).T == along
    hit = jnp.sum(jnp.where(named, 1.0, 0.0), axis=0, keepdims=True)
    row = jnp.sum(jnp.where(named, down, 0.0), axis=0, keepdims=True)
    return (row + (1.0 - hit) * count).astype(I32)


def index_kernel(where_ref, *rest, **sizes):
    inputs = rest[:8]
    info_ref, stacked_ref, wide_ref, narrow_ref = rest[9:13]
    locals_ = rest[13:21]
    sems = rest[21]
    copies = [pltpu.make_async_copy(a, b, sems.at[n]) for n, (a, b) in enumerate(zip(inputs, locals_))]
    for copy in copies:
        copy.start()
    for copy in copies:
        copy.wait()
    fill_tables(where_ref, *locals_, info_ref, stacked_ref, wide_ref, narrow_ref, **sizes)


def fill_tables(
    where_ref,
    cols_ref,
    slot_ref,
    owner_ref,
    place_ref,
    slot2_ref,
    owner2_ref,
    place2_ref,
    coarse_ref,
    info_ref,
    stacked_ref,
    wide_ref,
    narrow_ref,
    *,
    parts,
    capacity,
    capacity2,
    owned,
    owned2,
):
    region = where_ref[0]
    dom = where_ref[1]
    stencil, rows = cols_ref.shape
    rows2 = slot2_ref.shape[1]
    group = stencil + 1
    span = parts * rows
    first = region * span
    quarters_of(coarse_ref, stacked_ref, wide_ref)
    info_ref[0:group, :] = jnp.full((group, LANES), stencil * owned, I32)
    info_ref[group : 2 * group, :] = jnp.full((group, LANES), group * owned2, I32)
    info_ref[2 * group :, :] = jnp.full((group, LANES), dom, I32)
    info_ref[0:stencil, 0:rows] = slot_ref[...] * owned + place_ref[...]
    info_ref[group : group + stencil, 0:rows2] = place2_ref[...] * group + slot2_ref[...]
    cols = cols_ref[...]
    step = jnp.where(cols < first, 0, jnp.where(cols >= first + span, 2, 1))
    begin = ((region + step - 1) * parts + dom) * rows
    info_ref[2 * group : 2 * group + stencil, 0:rows] = (cols - begin) * 4 + table_of(step, region)
    info_ref[stencil : stencil + 1, :] = owner_order(owner_ref, narrow_ref, capacity)
    info_ref[group + stencil : 2 * group, :] = owner_order(owner2_ref, narrow_ref, capacity2)
    stacked_ref[rows2] = info_ref[0 : 2 * group, :].astype(F32).astype(BF16)


def terms_kernel(table_ref, blocks_ref, before_ref, own_ref, after_ref, *rest, offsets, capacity, waited):
    outs = rest[waited : waited + len(offsets)]
    info_ref, buffer_ref, info_sem, row_sem = rest[waited + len(offsets) :]
    stencil, width = buffer_ref.shape[1], buffer_ref.shape[2]
    half = width // 2
    narrow = LANES // 2
    flat = narrow * narrow // LANES

    table_copy = pltpu.make_async_copy(table_ref, info_ref, info_sem)
    table_copy.start()
    table_copy.wait()
    dom = info_ref[3 * (stencil + 1) - 1, 0]

    def source_of(offset, r):
        return jnp.minimum(info_ref[stencil, (dom ^ offset) * capacity + r], own_ref.shape[0] - 1)

    def row_copy(n, source):
        return pltpu.make_async_copy(blocks_ref.at[source], buffer_ref.at[n], row_sem.at[n])

    for n, offset in enumerate(offsets):
        for r in range(capacity):
            row_copy(n * capacity + r, source_of(offset, r)).start()

    left = low_lanes((half, LANES), narrow)
    left_flat = low_lanes((flat, LANES), narrow)
    out_row = lax.broadcasted_iota(I32, (narrow, LANES), 0)
    in_col = lax.broadcasted_iota(I32, (narrow, LANES), 1)
    chosen = jnp.where(out_row < flat, 2 * out_row, 2 * (out_row - flat) + 1)
    pick = jnp.where(in_col == chosen, 1.0, 0.0).astype(BF16)
    zero = jnp.zeros((half, LANES), BF16)

    def neighbour(source, k):
        code = info_ref[2 * (stencil + 1) + k, source]
        row = lax.shift_right_logical(code, 2)
        step = code & 3
        return jnp.where(step == 0, before_ref[row], jnp.where(step == 1, own_ref[row], after_ref[row]))

    def one_row(n, source, out_ref, r):
        mine = own_ref[source]
        column = jnp.concatenate([mine, pltpu.roll(mine, narrow, 1)], axis=0)
        turned = lax.dot_general(
            pick, column, (((1,), (1,)), ((), ())), preferred_element_type=F32
        ).astype(BF16)
        products = []
        for k in range(0, stencil, 2):
            one = neighbour(source, k)
            weights = [jnp.where(left, one, zero), jnp.where(left, pltpu.roll(one, narrow, 1), zero)]
            lhs = buffer_ref[n, k]
            if k + 1 < stencil:
                two = neighbour(source, k + 1)
                weights += [jnp.where(left, zero, pltpu.roll(two, narrow, 1)), jnp.where(left, zero, two)]
                lhs = jnp.concatenate([lhs, buffer_ref[n, k + 1]], axis=1)
            products.append(
                jnp.dot(lhs, jnp.concatenate(weights, axis=0), preferred_element_type=F32).astype(BF16)
            )
        term = jnp.dot(turned, jnp.concatenate(products, axis=1), preferred_element_type=F32)
        for k in range(0, stencil, 2):
            pair = term[:, k // 2 * LANES : (k // 2 + 1) * LANES]
            even = pair[:flat]
            odd = pair[flat:]
            base = (r * stencil + k) * flat
            out_ref[pl.ds(base, flat), :] = jnp.where(left_flat, even, pltpu.roll(odd, narrow, 1)).astype(BF16)
            if k + 1 < stencil:
                out_ref[pl.ds(base + flat, flat), :] = jnp.where(
                    left_flat, pltpu.roll(even, narrow, 1), odd
                ).astype(BF16)

    for n, offset in enumerate(offsets):
        sources = [source_of(offset, r) for r in range(capacity)]
        for r, source in enumerate(sources):
            row_copy(n * capacity + r, source).wait()
        for r, source in enumerate(sources):
            one_row(n * capacity + r, source, outs[n], r)


def level_one(info, blocks, before, own, after, offsets, capacity, waited):
    rows, stencil, width, _ = blocks.shape
    narrow = LANES // 2
    flat = narrow * narrow // LANES
    shape = jax.ShapeDtypeStruct((capacity * stencil * flat, LANES), BF16)
    count = len(offsets) * capacity
    return pl.pallas_call(
        functools.partial(terms_kernel, offsets=offsets, capacity=capacity, waited=len(waited)),
        out_shape=tuple(shape for _ in offsets),
        in_specs=[hbm(), hbm(), vmem(), vmem(), vmem()] + [hbm()] * len(waited),
        out_specs=tuple(vmem() for _ in offsets),
        scratch_shapes=[
            pltpu.SMEM(info.shape, I32),
            pltpu.VMEM((count, stencil, width, width), BF16),
            pltpu.SemaphoreType.DMA(()),
            pltpu.SemaphoreType.DMA((count,)),
        ],
        compiler_params=params(),
    )(
        pltpu.with_memory_space_constraint(info, pltpu.HBM),
        pltpu.with_memory_space_constraint(blocks, pltpu.HBM),
        before,
        own,
        after,
        *waited,
    )


def pick_kernel(index_ref, first_ref, own_ref, second_ref, mine_ref, waited_ref, out_ref, turned_ref):
    stencil, count = index_ref.shape
    quarter = LANES // 4
    narrow = LANES // 2

    def body(q, carry):
        for k in range(stencil):
            code = index_ref[k, q]
            row = lax.shift_right_logical(code, 2)
            step = code & 3
            out_ref[q * stencil + k] = jnp.where(
                step == 0, first_ref[row], jnp.where(step == 1, own_ref[row], second_ref[row])
            )
        return carry

    lax.fori_loop(0, count, body, 0, unroll=4)
    square = (LANES, LANES)
    row = lax.broadcasted_iota(I32, square, 0)
    lane = lax.broadcasted_iota(I32, square, 1)
    old = row // quarter * quarter + row % 8 * 4 + row % quarter // 8
    pick = jnp.where(lane == old, 1.0, 0.0).astype(BF16)
    new = lax.broadcasted_iota(I32, (narrow, narrow), 0)
    old = lax.broadcasted_iota(I32, (narrow, narrow), 1)
    order = jnp.where(old == new % quarter * 2 + new // quarter, 1.0, 0.0).astype(BF16)
    block = lax.broadcasted_iota(I32, (16, LANES), 1) // quarter
    columns = []
    for g in range(count // 4):
        pieces = []
        for h in range(4):
            total = None
            for n in range(4):
                shift = (n - h) % 4 * quarter
                piece = mine_ref[4 * g + n]
                piece = pltpu.roll(piece, shift, 1) if shift else piece
                total = piece if total is None else jnp.where(block == n, piece, total)
            pieces.append(total)
        columns.append(jnp.concatenate(pieces, axis=0))
    ordered = [jnp.dot(order, column, preferred_element_type=F32).astype(BF16) for column in columns]
    for g, column in enumerate(ordered):
        turned = lax.dot_general(pick, column, (((1,), (1,)), ((), ())), preferred_element_type=F32).astype(BF16)
        for n in range(4):
            turned_ref[4 * g + n] = turned[n * quarter : (n + 1) * quarter]


def pick_rows(index, first, own, second, mine, waited):
    stencil, count = index.shape
    return pl.pallas_call(
        pick_kernel,
        out_shape=(
            jax.ShapeDtypeStruct((count * stencil,) + own.shape[1:], own.dtype),
            jax.ShapeDtypeStruct((count, LANES // 4, LANES // 2), own.dtype),
        ),
        in_specs=[smem(), vmem(), vmem(), vmem(), vmem(), hbm()],
        out_specs=(vmem(), vmem()),
        compiler_params=params(),
    )(index, first, own, second, mine, waited)


def add_terms(part_ref, target_of, sum_ref, capacity, stencil):
    flat = sum_ref.shape[1]
    for r in range(capacity):
        for k in range(stencil):
            term = part_ref[pl.ds((r * stencil + k) * flat, flat), :].astype(F32)
            sum_ref[target_of(r, k)] += term


def early_kernel(where_ref, table_ref, *rest, soon, late, parts, capacity, capacity2, owned, stencil):
    sum_ref, lists_ref = rest[-2:]
    dom = where_ref[1]
    group = stencil + 1

    def row_of(d, level, slot):
        return table_ref[((dom ^ d) * 2 + level) * group + stencil, slot]

    def target_at(d, level, row, k):
        return table_ref[((dom ^ d) * 2 + level) * group + k, row]

    at = 0
    for d in range(parts):
        for r in range(capacity2):
            row = table_ref[(dom * 2 + 2) * group - 1, (dom ^ d) * capacity2 + r]
            lists_ref[at] = jnp.minimum(row, owned - 1)
            at += 1
    for d in late:
        for r in range(capacity):
            row = row_of(d, 0, dom * capacity + r)
            for k in range(stencil):
                lists_ref[at] = target_at(d, 0, row, k)
                at += 1
    for d in range(parts):
        for r in range(capacity2):
            row = row_of(d, 1, dom * capacity2 + r)
            for k in range(stencil):
                lists_ref[at] = target_at(d, 1, row, k)
                at += 1
    sum_ref[...] = jnp.zeros(sum_ref.shape, F32)
    for d, part_ref in zip(soon, rest):
        rows = [row_of(d, 0, dom * capacity + r) for r in range(capacity)]
        add_terms(part_ref, lambda r, k: target_at(d, 0, rows[r], k), sum_ref, capacity, stencil)


def early_sums(where, table, waited, arrived, soon, late, parts, capacity, capacity2, owned, stencil):
    sizes = dict(parts=parts, capacity=capacity, capacity2=capacity2, owned=owned, stencil=stencil)
    count = parts * capacity2 * (stencil + 1) + len(late) * capacity * stencil
    return pl.pallas_call(
        functools.partial(early_kernel, soon=soon, late=late, **sizes),
        out_shape=(
            jax.ShapeDtypeStruct((stencil * owned + 1, LANES // 4, LANES), F32),
            jax.ShapeDtypeStruct((count,), I32),
        ),
        in_specs=[smem(), smem()] + [vmem()] * len(soon) + [hbm()],
        out_specs=(vmem(), smem()),
        compiler_params=params(),
    )(where, table, *arrived, waited)


def owner_kernel(
    lists_ref,
    picked_ref,
    own_ref,
    early_ref,
    *rest,
    parts,
    offsets,
    capacity,
    capacity2,
    owned,
    stencil,
):
    arrived = rest[: len(offsets)]
    out_ref = rest[len(offsets)]
    sum_ref = rest[len(offsets) + 1]
    sends = rest[len(offsets) + 2 : len(offsets) + 2 + parts]
    (term_ref,) = rest[len(offsets) + 2 + parts :]
    flat = sum_ref.shape[1]
    narrow = LANES // 2
    for n, part_ref in enumerate(arrived):
        first = parts * capacity2 + n * capacity * stencil
        add_terms(part_ref, lambda r, k: lists_ref[first + r * stencil + k], sum_ref, capacity, stencil)

    left = low_lanes((flat, LANES), narrow)
    quarter = LANES // 4
    eighth = lax.broadcasted_iota(I32, (8, LANES), 1) // quarter
    block = lax.broadcasted_iota(I32, (16, LANES), 1) // quarter
    none = jnp.zeros((16, LANES), BF16)

    batch = 2

    def second(step, carry):
        places = [(step * batch + n, r) for n in range(batch) for r in range(capacity2)]
        names = [lists_ref[d * capacity2 + r] for d, r in places]
        products = []
        for q in names:
            rows = []
            weights = []
            for k in range(0, stencil, 2):
                one = sum_ref[k * owned + q].astype(BF16)
                out_ref[k * owned + q] = one
                if k + 1 < stencil:
                    two = sum_ref[(k + 1) * owned + q].astype(BF16)
                    out_ref[(k + 1) * owned + q] = two
                else:
                    two = jnp.zeros((flat, LANES), BF16)
                even = jnp.where(left, one, pltpu.roll(two, narrow, 1))
                odd = jnp.where(left, pltpu.roll(one, narrow, 1), two)
                rows.append(jnp.concatenate([even, odd], axis=0))
            for k in range(stencil):
                packed = picked_ref[q * stencil + k]
                for h in range(4):
                    shift = (k - h) % 4 * quarter
                    turned = pltpu.roll(packed, shift, 1) if shift else packed
                    weights.append(jnp.where(block == k % 4, turned, none))
            groups = []
            for g in range((stencil + 3) // 4):
                lhs = jnp.concatenate(rows[2 * g : 2 * g + 2], axis=1)
                rhs = jnp.concatenate(weights[16 * g : 16 * g + 16], axis=0)
                product = jnp.dot(lhs[:, : rhs.shape[0]], rhs, preferred_element_type=F32)
                groups.append(product.astype(BF16))
            products.append(jnp.concatenate(groups, axis=1))
        terms = [jnp.dot(own_ref[q], p, preferred_element_type=F32) for q, p in zip(names, products)]
        for (d, r), term in zip(places, terms):
            for k in range(stencil):
                g = k // 4
                total = None
                for w in range(4):
                    piece = term[w * 8 : (w + 1) * 8, g * LANES : (g + 1) * LANES]
                    shift = (w - k) % 4 * quarter
                    if shift:
                        piece = pltpu.roll(piece, shift, 1)
                    total = piece if total is None else jnp.where(eighth == w, piece, total)
                term_ref[d, pl.ds((r * stencil + k) * 8, 8), :] = total
        return carry

    lax.fori_loop(0, parts // batch, second, 0)
    for d in range(parts):
        sends[d][...] = term_ref[d].astype(BF16)


def owner_level(lists, picked, own, early, arrived, offsets, parts, capacity, capacity2, owned, stencil):
    flat = LANES // 4
    send = jax.ShapeDtypeStruct((capacity2 * stencil * 8, LANES), BF16)
    return pl.pallas_call(
        functools.partial(
            owner_kernel,
            parts=parts,
            offsets=offsets,
            capacity=capacity,
            capacity2=capacity2,
            owned=owned,
            stencil=stencil,
        ),
        out_shape=(
            jax.ShapeDtypeStruct((stencil * owned, flat, LANES), BF16),
            jax.ShapeDtypeStruct(early.shape, F32),
        )
        + (send,) * parts,
        in_specs=[smem()] + [vmem()] * (3 + len(offsets)),
        out_specs=(vmem(),) * (2 + parts),
        scratch_shapes=[pltpu.VMEM((parts, capacity2 * stencil * 8, LANES), F32)],
        input_output_aliases={3: 1},
        compiler_params=params(),
    )(lists, picked, own, early, *arrived)


def final_kernel(lists_ref, *rest, parts, capacity2, stencil):
    arrived = rest[:parts][::-1]
    out_ref = rest[parts]
    sum_ref, other_ref = rest[parts + 1 :]
    deep = stencil + 1
    first = lists_ref.shape[0] - parts * capacity2 * stencil
    other_ref[...] = jnp.zeros(other_ref.shape, F32)
    sum_ref[...] = jnp.zeros(sum_ref.shape, F32)
    for d in range(0, parts, 2):
        pairs = [(sum_ref, d), (other_ref, d + 1)]
        values = [arrived[e][...].astype(F32) for _, e in pairs]
        for r in range(capacity2):
            for k in range(stencil):
                at = r * stencil + k
                for (into_ref, e), value in zip(pairs, values):
                    target = lists_ref[first + e * capacity2 * stencil + at]
                    into_ref[target] += value[at * 8 : (at + 1) * 8]
    for u in range(out_ref.shape[0]):
        for t in range(8):
            tile = sum_ref[pl.ds(u * deep, deep), t, :] + other_ref[pl.ds(u * deep, deep), t, :]
            out_ref[u, :, pl.ds(t * LANES, LANES)] = tile[:stencil].astype(BF16)


def final_level(lists, arrived, parts, capacity2, owned2, stencil):
    return pl.pallas_call(
        functools.partial(final_kernel, parts=parts, capacity2=capacity2, stencil=stencil),
        out_shape=jax.ShapeDtypeStruct((owned2, stencil, 8 * LANES), BF16),
        in_specs=[smem()] + [vmem()] * parts,
        out_specs=vmem(),
        scratch_shapes=[pltpu.VMEM((owned2 * (stencil + 1) + 1, 8, LANES), F32)] * 2,
        compiler_params=params(),
    )(lists, *arrived[::-1])


def chunks_of(parts):
    order = sorted(range(parts), key=lambda d: (-(d >> 1).bit_count(), -(d & 1), -d))
    return [tuple(order[i : i + 2]) for i in range(0, parts, 2)]


def local(
    fine_blocks,
    interp,
    fine_cols,
    fine_slot,
    fine_owner,
    fine_place,
    coarse_interp,
    coarse_cols,
    coarse_slot,
    coarse_owner,
    coarse_place,
):
    rows, stencil, width, _ = fine_blocks.shape
    narrow = interp.shape[1] // width
    parts = lax.axis_size("dom")
    region = lax.axis_index("region")
    dom = lax.axis_index("dom")
    owned = rows // 2
    owned2 = owned // 2
    capacity = max(2, rows // 8)
    capacity2 = max(2, owned // 8)
    where = jnp.stack([region, dom]).astype(I32)

    own = halves(interp)
    halo = neighbours(own, "region")

    size2 = coarse_interp.shape[1]
    group = stencil + 1
    inputs = [
        fine_cols.T,
        fine_slot.T,
        fine_owner.T,
        fine_place.reshape(1, rows),
        coarse_slot.T,
        coarse_owner.T,
        coarse_place.reshape(1, owned),
        coarse_interp,
    ]
    info, stacked = pl.pallas_call(
        functools.partial(
            index_kernel, parts=parts, capacity=capacity, capacity2=capacity2, owned=owned, owned2=owned2
        ),
        out_shape=(
            jax.ShapeDtypeStruct((3 * group, LANES), I32),
            jax.ShapeDtypeStruct((owned + 1, size2 // LANES, LANES), BF16),
        ),
        in_specs=[smem()] + [hbm()] * 9,
        out_specs=(vmem(), vmem()),
        scratch_shapes=[pltpu.VMEM((coarse_interp.size // LANES, LANES), F32), pltpu.VMEM((8, LANES), F32)]
        + [pltpu.VMEM(x.shape, x.dtype) for x in inputs]
        + [pltpu.SemaphoreType.DMA((len(inputs),))],
        compiler_params=params(),
    )(where, *[pltpu.with_memory_space_constraint(x, pltpu.HBM) for x in inputs], own)

    table = lax.all_gather(stacked, "dom", axis=0, tiled=True)
    pitch = owned + 1
    targets = table.reshape((parts, pitch, 2 * group, LANES))[:, owned].reshape(parts * 2 * group, LANES).astype(I32)

    tables = neighbours(table, "region")
    arrived = [None] * parts
    chunks = chunks_of(parts)
    sent = ()
    for n, offsets in enumerate(chunks):
        waited = tuple(sent[:1])
        if n == 2:
            waited = waited + tables
        if n >= 3:
            waited = waited + tuple(arrived[d] for d in chunks[n - 3])
        sent = level_one(info, fine_blocks, halo[0], own, halo[1], offsets, capacity, waited)
        for offset, cells in zip(offsets, sent):
            arrived[offset] = exchange(cells, "dom", offset) if offset else cells
    span2 = parts * owned
    inside = coarse_cols % span2
    step2 = table_of(coarse_cols // span2 - region + 1, region)
    index2 = (inside // owned * pitch + inside % owned) * 4 + step2
    picked, turned = pick_rows(index2.T, tables[0], table, tables[1], stacked, sent[0])
    soon = list(chunks[-1]) + [d for offsets in chunks[: len(chunks) // 2] for d in offsets]
    late = [d for d in range(parts) if d not in soon]
    early, lists = early_sums(
        where,
        targets,
        picked,
        [arrived[d] for d in soon],
        soon,
        late,
        parts,
        capacity,
        capacity2,
        owned,
        stencil,
    )
    outs = owner_level(
        lists,
        picked,
        turned,
        early,
        [arrived[d] for d in late],
        late,
        parts,
        capacity,
        capacity2,
        owned,
        stencil,
    )
    coarse_blocks = outs[0].reshape(stencil, owned, narrow * narrow).transpose(1, 0, 2)
    arrived2 = list(outs[2:])
    for d in range(parts - 1, 0, -1):
        arrived2[d] = exchange(arrived2[d], "dom", d)
    second = final_level(lists, arrived2, parts, capacity2, owned2, stencil)
    return (coarse_blocks, second)


def solution(mesh):
    in_specs = (
        P(("region", "dom"), None, None, None),
        P(("region", "dom"), None),
        P(("region", "dom"), None),
        P(("region", "dom"), None),
        P(("region", "dom"), None),
        P(("region", "dom")),
        P(("region", "dom"), None),
        P(("region", "dom"), None),
        P(("region", "dom"), None),
        P(("region", "dom"), None),
        P(("region", "dom")),
    )
    out_specs = (P(("region", "dom"), None, None), P(("region", "dom"), None, None))
    return jax.shard_map(local, mesh=mesh, in_specs=in_specs, out_specs=out_specs, check_vma=False)
```

```python
import functools

import jax
import jax.numpy as jnp
from jax import lax
from jax.experimental import pallas as pl
from jax.experimental.pallas import tpu as pltpu
from jax.sharding import PartitionSpec as P

BF16 = jnp.bfloat16
F32 = jnp.float32
I32 = jnp.int32
LANES = 128
VMEM_LIMIT = 32 * 1024 * 1024


def vmem():
    return pl.BlockSpec(memory_space=pltpu.VMEM)


def smem():
    return pl.BlockSpec(memory_space=pltpu.SMEM)


def hbm():
    return pl.BlockSpec(memory_space=pl.ANY)


def params():
    return pltpu.CompilerParams(vmem_limit_bytes=VMEM_LIMIT)


def low_lanes(shape, bound):
    return lax.broadcasted_iota(I32, shape, len(shape) - 1) < bound


def exchange(cells, axis, offset):
    count = lax.axis_size(axis)
    return lax.ppermute(cells, axis, [(i, i ^ offset) for i in range(count)])


def partner(index, odd, count):
    other = ((index + odd) ^ 1) - odd
    return other if 0 <= other < count else index


def neighbours(cells, axis):
    count = lax.axis_size(axis)
    return tuple(lax.ppermute(cells, axis, [(i, partner(i, odd, count)) for i in range(count)]) for odd in (1, 0))


def table_of(step, region):
    swapped = jnp.where(region % 2 == 0, step, 2 - step)
    return jnp.where(step == 1, 1, swapped)


def halves_kernel(flat_ref, out_ref, rows_ref, wide_ref, sems):
    steps, group = rows_ref.shape[:2]
    deep = rows_ref.shape[2] // LANES
    half = deep // 2
    left = low_lanes((group, LANES), LANES // 2)

    def copy(g):
        return pltpu.make_async_copy(flat_ref.at[pl.ds(g * group, group)], rows_ref.at[g], sems.at[g])

    for g in range(steps):
        copy(g).start()
    for g in range(steps):
        copy(g).wait()
        for t in range(half):
            upper = rows_ref[g, :, pl.ds(t * LANES, LANES)].astype(F32)
            lower = rows_ref[g, :, pl.ds((t + half) * LANES, LANES)].astype(F32)
            even = jnp.where(left, upper, pltpu.roll(lower, LANES // 2, 1))
            odd = jnp.where(left, pltpu.roll(upper, LANES // 2, 1), lower)
            wide_ref[g, pl.ds(2 * t, group, stride=deep), :] = even
            wide_ref[g, pl.ds(2 * t + 1, group, stride=deep), :] = odd
        for r in range(group):
            out_ref[g * group + r] = wide_ref[g, pl.ds(r * deep, deep), :].astype(BF16)


def halves(flat):
    rows, size = flat.shape
    deep = size // LANES
    group = 16
    steps = rows // group
    return pl.pallas_call(
        halves_kernel,
        out_shape=jax.ShapeDtypeStruct((rows, deep, LANES), BF16),
        in_specs=[pl.BlockSpec(memory_space=pltpu.HBM)],
        out_specs=vmem(),
        scratch_shapes=[
            pltpu.VMEM((steps, group, size), BF16),
            pltpu.VMEM((steps, group * deep, LANES), F32),
            pltpu.SemaphoreType.DMA((steps,)),
        ],
        compiler_params=params(),
    )(pltpu.with_memory_space_constraint(flat, pltpu.HBM))


def quarters_of(coarse_ref, quarters_ref, wide_ref):
    count = coarse_ref.shape[0]
    deep = coarse_ref.shape[1] // LANES
    quarter = LANES // 4
    lane = lax.broadcasted_iota(I32, (count, LANES), 1) // quarter
    for t in range(deep // 4):
        tiles = [coarse_ref[:, pl.ds((h * deep // 4 + t) * LANES, LANES)].astype(F32) for h in range(4)]
        for u in range(4):
            total = None
            for h in range(4):
                shift = (h - u) % 4 * quarter
                piece = pltpu.roll(tiles[h], shift, 1) if shift else tiles[h]
                total = piece if total is None else jnp.where(lane == h, piece, total)
            wide_ref[pl.ds(4 * t + u, count, stride=deep), :] = total
    for r in range(count):
        quarters_ref[r] = wide_ref[pl.ds(r * deep, deep), :].astype(BF16)


def owner_order(owner_ref, wide_ref, capacity):
    count = owner_ref.shape[1]
    square = (LANES, LANES)
    down = lax.broadcasted_iota(I32, square, 0).astype(F32)
    along = lax.broadcasted_iota(I32, square, 1).astype(F32)
    wide_ref[...] = jnp.full(wide_ref.shape, -1.0, F32)
    wide_ref[0:1, 0:count] = owner_ref[...].astype(F32)
    owner = wide_ref[0:1, :]
    across = jnp.broadcast_to(owner, square)
    earlier = jnp.where((across == across.T) & (down < along), 1.0, 0.0)
    rank = jnp.sum(earlier, axis=0, keepdims=True)
    position = jnp.where(owner >= 0.0, owner * capacity + rank, -1.0)
    named = jnp.broadcast_to(position, square).T == along
    hit = jnp.sum(jnp.where(named, 1.0, 0.0), axis=0, keepdims=True)
    row = jnp.sum(jnp.where(named, down, 0.0), axis=0, keepdims=True)
    return (row + (1.0 - hit) * count).astype(I32)


def index_kernel(where_ref, *rest, **sizes):
    inputs = rest[:8]
    info_ref, stacked_ref, wide_ref, narrow_ref = rest[9:13]
    locals_ = rest[13:21]
    sems = rest[21]
    copies = [pltpu.make_async_copy(a, b, sems.at[n]) for n, (a, b) in enumerate(zip(inputs, locals_))]
    for copy in copies:
        copy.start()
    for copy in copies:
        copy.wait()
    fill_tables(where_ref, *locals_, info_ref, stacked_ref, wide_ref, narrow_ref, **sizes)


def fill_tables(
    where_ref,
    cols_ref,
    slot_ref,
    owner_ref,
    place_ref,
    slot2_ref,
    owner2_ref,
    place2_ref,
    coarse_ref,
    info_ref,
    stacked_ref,
    wide_ref,
    narrow_ref,
    *,
    parts,
    capacity,
    capacity2,
    owned,
    owned2,
):
    region = where_ref[0]
    dom = where_ref[1]
    stencil, rows = cols_ref.shape
    rows2 = slot2_ref.shape[1]
    group = stencil + 1
    span = parts * rows
    first = region * span
    quarters_of(coarse_ref, stacked_ref, wide_ref)
    info_ref[0:group, :] = jnp.full((group, LANES), stencil * owned, I32)
    info_ref[group : 2 * group, :] = jnp.full((group, LANES), group * owned2, I32)
    info_ref[2 * group :, :] = jnp.full((group, LANES), dom, I32)
    info_ref[0:stencil, 0:rows] = slot_ref[...] * owned + place_ref[...]
    info_ref[group : group + stencil, 0:rows2] = place2_ref[...] * group + slot2_ref[...]
    cols = cols_ref[...]
    step = jnp.where(cols < first, 0, jnp.where(cols >= first + span, 2, 1))
    begin = ((region + step - 1) * parts + dom) * rows
    info_ref[2 * group : 2 * group + stencil, 0:rows] = (cols - begin) * 4 + table_of(step, region)
    info_ref[stencil : stencil + 1, :] = owner_order(owner_ref, narrow_ref, capacity)
    info_ref[group + stencil : 2 * group, :] = owner_order(owner2_ref, narrow_ref, capacity2)
    stacked_ref[rows2] = info_ref[0 : 2 * group, :].astype(F32).astype(BF16)


def terms_kernel(info_ref, blocks_ref, before_ref, own_ref, after_ref, *rest, offsets, capacity, waited):
    outs = rest[waited : waited + len(offsets)]
    buffer_ref, row_sem = rest[waited + len(offsets) :]
    stencil, width = buffer_ref.shape[1], buffer_ref.shape[2]
    half = width // 2
    narrow = LANES // 2
    flat = narrow * narrow // LANES

    dom = info_ref[3 * (stencil + 1) - 1, 0]

    def source_of(offset, r):
        return jnp.minimum(info_ref[stencil, (dom ^ offset) * capacity + r], own_ref.shape[0] - 1)

    def row_copy(n, source):
        return pltpu.make_async_copy(blocks_ref.at[source], buffer_ref.at[n], row_sem.at[n])

    def fetch(n):
        for r in range(capacity):
            row_copy(n * capacity + r, source_of(offsets[n], r)).start()

    fetch(0)
    left = low_lanes((half, LANES), narrow)
    left_flat = low_lanes((flat, LANES), narrow)
    out_row = lax.broadcasted_iota(I32, (narrow, LANES), 0)
    in_col = lax.broadcasted_iota(I32, (narrow, LANES), 1)
    chosen = jnp.where(out_row < flat, 2 * out_row, 2 * (out_row - flat) + 1)
    pick = jnp.where(in_col == chosen, 1.0, 0.0).astype(BF16)
    zero = jnp.zeros((half, LANES), BF16)

    def neighbour(source, k):
        code = info_ref[2 * (stencil + 1) + k, source]
        row = lax.shift_right_logical(code, 2)
        step = code & 3
        return jnp.where(step == 0, before_ref[row], jnp.where(step == 1, own_ref[row], after_ref[row]))

    def one_row(n, source, out_ref, r):
        mine = own_ref[source]
        column = jnp.concatenate([mine, pltpu.roll(mine, narrow, 1)], axis=0)
        turned = lax.dot_general(
            pick, column, (((1,), (1,)), ((), ())), preferred_element_type=F32
        ).astype(BF16)
        products = []
        for k in range(0, stencil, 2):
            one = neighbour(source, k)
            weights = [jnp.where(left, one, zero), jnp.where(left, pltpu.roll(one, narrow, 1), zero)]
            lhs = buffer_ref[n, k]
            if k + 1 < stencil:
                two = neighbour(source, k + 1)
                weights += [jnp.where(left, zero, pltpu.roll(two, narrow, 1)), jnp.where(left, zero, two)]
                lhs = jnp.concatenate([lhs, buffer_ref[n, k + 1]], axis=1)
            products.append(
                jnp.dot(lhs, jnp.concatenate(weights, axis=0), preferred_element_type=F32).astype(BF16)
            )
        term = jnp.dot(turned, jnp.concatenate(products, axis=1), preferred_element_type=F32)
        for k in range(0, stencil, 2):
            pair = term[:, k // 2 * LANES : (k // 2 + 1) * LANES]
            even = pair[:flat].astype(BF16)
            odd = pair[flat:].astype(BF16)
            base = (r * stencil + k) * flat
            out_ref[pl.ds(base, flat), :] = jnp.where(left_flat, even, pltpu.roll(odd, narrow, 1))
            if k + 1 < stencil:
                out_ref[pl.ds(base + flat, flat), :] = jnp.where(left_flat, pltpu.roll(even, narrow, 1), odd)

    for n, offset in enumerate(offsets):
        sources = [source_of(offset, r) for r in range(capacity)]
        for r, source in enumerate(sources):
            row_copy(n * capacity + r, source).wait()
        if n + 1 < len(offsets):
            fetch(n + 1)
        for r, source in enumerate(sources):
            one_row(n * capacity + r, source, outs[n], r)


def level_one(info, blocks, before, own, after, offsets, capacity, waited):
    rows, stencil, width, _ = blocks.shape
    narrow = LANES // 2
    flat = narrow * narrow // LANES
    shape = jax.ShapeDtypeStruct((capacity * stencil * flat, LANES), BF16)
    count = len(offsets) * capacity
    return pl.pallas_call(
        functools.partial(terms_kernel, offsets=offsets, capacity=capacity, waited=len(waited)),
        out_shape=tuple(shape for _ in offsets),
        in_specs=[smem(), hbm(), vmem(), vmem(), vmem()] + [hbm()] * len(waited),
        out_specs=tuple(vmem() for _ in offsets),
        scratch_shapes=[
            pltpu.VMEM((count, stencil, width, width), BF16),
            pltpu.SemaphoreType.DMA((count,)),
        ],
        compiler_params=params(),
    )(
        info,
        pltpu.with_memory_space_constraint(blocks, pltpu.HBM),
        before,
        own,
        after,
        *waited,
    )


def pick_kernel(index_ref, first_ref, own_ref, second_ref, mine_ref, waited_ref, out_ref, turned_ref):
    stencil, count = index_ref.shape
    quarter = LANES // 4
    narrow = LANES // 2

    def body(q, carry):
        for k in range(stencil):
            code = index_ref[k, q]
            row = lax.shift_right_logical(code, 2)
            step = code & 3
            out_ref[q * stencil + k] = jnp.where(
                step == 0, first_ref[row], jnp.where(step == 1, own_ref[row], second_ref[row])
            )
        return carry

    lax.fori_loop(0, count, body, 0, unroll=4)
    square = (LANES, LANES)
    row = lax.broadcasted_iota(I32, square, 0)
    lane = lax.broadcasted_iota(I32, square, 1)
    old = row // quarter * quarter + row % 8 * 4 + row % quarter // 8
    pick = jnp.where(lane == old, 1.0, 0.0).astype(BF16)
    new = lax.broadcasted_iota(I32, (narrow, narrow), 0)
    old = lax.broadcasted_iota(I32, (narrow, narrow), 1)
    order = jnp.where(old == new % quarter * 2 + new // quarter, 1.0, 0.0).astype(BF16)
    block = lax.broadcasted_iota(I32, (16, LANES), 1) // quarter
    columns = []
    for g in range(count // 4):
        pieces = []
        for h in range(4):
            total = None
            for n in range(4):
                shift = (n - h) % 4 * quarter
                piece = mine_ref[4 * g + n]
                piece = pltpu.roll(piece, shift, 1) if shift else piece
                total = piece if total is None else jnp.where(block == n, piece, total)
            pieces.append(total)
        columns.append(jnp.concatenate(pieces, axis=0))
    ordered = [jnp.dot(order, column, preferred_element_type=F32).astype(BF16) for column in columns]
    for g, column in enumerate(ordered):
        turned = lax.dot_general(pick, column, (((1,), (1,)), ((), ())), preferred_element_type=F32).astype(BF16)
        for n in range(4):
            turned_ref[4 * g + n] = turned[n * quarter : (n + 1) * quarter]


def pick_rows(index, first, own, second, mine, waited):
    stencil, count = index.shape
    return pl.pallas_call(
        pick_kernel,
        out_shape=(
            jax.ShapeDtypeStruct((count * stencil,) + own.shape[1:], own.dtype),
            jax.ShapeDtypeStruct((count, LANES // 4, LANES // 2), own.dtype),
        ),
        in_specs=[smem(), vmem(), vmem(), vmem(), vmem(), hbm()],
        out_specs=(vmem(), vmem()),
        compiler_params=params(),
    )(index, first, own, second, mine, waited)


def add_terms(part_ref, target_of, sum_ref, capacity, stencil):
    flat = sum_ref.shape[1]
    for r in range(capacity):
        for k in range(stencil):
            term = part_ref[pl.ds((r * stencil + k) * flat, flat), :].astype(F32)
            sum_ref[target_of(r, k)] += term


def early_kernel(where_ref, table_ref, *rest, soon, late, parts, capacity, capacity2, owned, stencil):
    sum_ref, lists_ref = rest[-2:]
    dom = where_ref[1]
    group = stencil + 1

    def row_of(d, level, slot):
        return table_ref[((dom ^ d) * 2 + level) * group + stencil, slot]

    def target_at(d, level, row, k):
        return table_ref[((dom ^ d) * 2 + level) * group + k, row]

    at = 0
    for d in range(parts):
        for r in range(capacity2):
            row = table_ref[(dom * 2 + 2) * group - 1, (dom ^ d) * capacity2 + r]
            lists_ref[at] = jnp.minimum(row, owned - 1)
            at += 1
    for d in late:
        for r in range(capacity):
            row = row_of(d, 0, dom * capacity + r)
            for k in range(stencil):
                lists_ref[at] = target_at(d, 0, row, k)
                at += 1
    for d in range(parts):
        for r in range(capacity2):
            row = row_of(d, 1, dom * capacity2 + r)
            for k in range(stencil):
                lists_ref[at] = target_at(d, 1, row, k)
                at += 1
    sum_ref[...] = jnp.zeros(sum_ref.shape, F32)
    for d, part_ref in zip(soon, rest):
        rows = [row_of(d, 0, dom * capacity + r) for r in range(capacity)]
        add_terms(part_ref, lambda r, k: target_at(d, 0, rows[r], k), sum_ref, capacity, stencil)


def early_sums(where, table, waited, arrived, soon, late, parts, capacity, capacity2, owned, stencil):
    sizes = dict(parts=parts, capacity=capacity, capacity2=capacity2, owned=owned, stencil=stencil)
    count = parts * capacity2 * (stencil + 1) + len(late) * capacity * stencil
    return pl.pallas_call(
        functools.partial(early_kernel, soon=soon, late=late, **sizes),
        out_shape=(
            jax.ShapeDtypeStruct((stencil * owned + 1, LANES // 4, LANES), F32),
            jax.ShapeDtypeStruct((count,), I32),
        ),
        in_specs=[smem(), smem()] + [vmem()] * len(soon) + [hbm()],
        out_specs=(vmem(), smem()),
        compiler_params=params(),
    )(where, table, *arrived, waited)


def owner_kernel(
    lists_ref,
    picked_ref,
    own_ref,
    early_ref,
    *rest,
    parts,
    offsets,
    capacity,
    capacity2,
    owned,
    stencil,
):
    arrived = rest[: len(offsets)]
    out_ref = rest[len(offsets)]
    sum_ref = rest[len(offsets) + 1]
    sends = rest[len(offsets) + 2 : len(offsets) + 2 + parts]
    (term_ref,) = rest[len(offsets) + 2 + parts :]
    flat = sum_ref.shape[1]
    narrow = LANES // 2
    for n, part_ref in enumerate(arrived):
        first = parts * capacity2 + n * capacity * stencil
        add_terms(part_ref, lambda r, k: lists_ref[first + r * stencil + k], sum_ref, capacity, stencil)

    left = low_lanes((flat, LANES), narrow)
    quarter = LANES // 4
    eighth = lax.broadcasted_iota(I32, (8, LANES), 1) // quarter
    block = lax.broadcasted_iota(I32, (16, LANES), 1) // quarter
    none = jnp.zeros((16, LANES), BF16)

    batch = 2

    def second(step, carry):
        places = [(step * batch + n, r) for n in range(batch) for r in range(capacity2)]
        names = [lists_ref[d * capacity2 + r] for d, r in places]
        products = []
        for q in names:
            rows = []
            weights = []
            for k in range(0, stencil, 2):
                one = sum_ref[k * owned + q].astype(BF16)
                out_ref[k * owned + q] = one
                if k + 1 < stencil:
                    two = sum_ref[(k + 1) * owned + q].astype(BF16)
                    out_ref[(k + 1) * owned + q] = two
                else:
                    two = jnp.zeros((flat, LANES), BF16)
                even = jnp.where(left, one, pltpu.roll(two, narrow, 1))
                odd = jnp.where(left, pltpu.roll(one, narrow, 1), two)
                rows.append(jnp.concatenate([even, odd], axis=0))
            for k in range(stencil):
                packed = picked_ref[q * stencil + k]
                for h in range(4):
                    shift = (k - h) % 4 * quarter
                    turned = pltpu.roll(packed, shift, 1) if shift else packed
                    weights.append(jnp.where(block == k % 4, turned, none))
            groups = []
            for g in range((stencil + 3) // 4):
                lhs = jnp.concatenate(rows[2 * g : 2 * g + 2], axis=1)
                rhs = jnp.concatenate(weights[16 * g : 16 * g + 16], axis=0)
                product = jnp.dot(lhs[:, : rhs.shape[0]], rhs, preferred_element_type=F32)
                groups.append(product.astype(BF16))
            products.append(jnp.concatenate(groups, axis=1))
        terms = [jnp.dot(own_ref[q], p, preferred_element_type=F32) for q, p in zip(names, products)]
        for (d, r), term in zip(places, terms):
            for k in range(stencil):
                g = k // 4
                total = None
                for w in range(4):
                    piece = term[w * 8 : (w + 1) * 8, g * LANES : (g + 1) * LANES]
                    shift = (w - k) % 4 * quarter
                    if shift:
                        piece = pltpu.roll(piece, shift, 1)
                    total = piece if total is None else jnp.where(eighth == w, piece, total)
                term_ref[d, pl.ds((r * stencil + k) * 8, 8), :] = total
        return carry

    lax.fori_loop(0, parts // batch, second, 0)
    for d in range(parts):
        sends[d][...] = term_ref[d].astype(BF16)


def owner_level(lists, picked, own, early, arrived, offsets, parts, capacity, capacity2, owned, stencil):
    flat = LANES // 4
    send = jax.ShapeDtypeStruct((capacity2 * stencil * 8, LANES), BF16)
    return pl.pallas_call(
        functools.partial(
            owner_kernel,
            parts=parts,
            offsets=offsets,
            capacity=capacity,
            capacity2=capacity2,
            owned=owned,
            stencil=stencil,
        ),
        out_shape=(
            jax.ShapeDtypeStruct((stencil * owned, flat, LANES), BF16),
            jax.ShapeDtypeStruct(early.shape, F32),
        )
        + (send,) * parts,
        in_specs=[smem()] + [vmem()] * (3 + len(offsets)),
        out_specs=(vmem(),) * (2 + parts),
        scratch_shapes=[pltpu.VMEM((parts, capacity2 * stencil * 8, LANES), F32)],
        input_output_aliases={3: 1},
        compiler_params=params(),
    )(lists, picked, own, early, *arrived)


def final_kernel(lists_ref, *rest, parts, capacity2, stencil):
    arrived = rest[:parts][::-1]
    out_ref = rest[parts]
    sum_ref, other_ref = rest[parts + 1 :]
    deep = stencil + 1
    first = lists_ref.shape[0] - parts * capacity2 * stencil
    other_ref[...] = jnp.zeros(other_ref.shape, F32)
    sum_ref[...] = jnp.zeros(sum_ref.shape, F32)
    for d in range(0, parts, 2):
        pairs = [(sum_ref, d), (other_ref, d + 1)]
        values = [arrived[e][...].astype(F32) for _, e in pairs]
        for r in range(capacity2):
            for k in range(stencil):
                at = r * stencil + k
                for (into_ref, e), value in zip(pairs, values):
                    target = lists_ref[first + e * capacity2 * stencil + at]
                    into_ref[target] += value[at * 8 : (at + 1) * 8]
    for u in range(out_ref.shape[0]):
        for t in range(8):
            tile = sum_ref[pl.ds(u * deep, deep), t, :] + other_ref[pl.ds(u * deep, deep), t, :]
            out_ref[u, :, pl.ds(t * LANES, LANES)] = tile[:stencil].astype(BF16)


def final_level(lists, arrived, parts, capacity2, owned2, stencil):
    return pl.pallas_call(
        functools.partial(final_kernel, parts=parts, capacity2=capacity2, stencil=stencil),
        out_shape=jax.ShapeDtypeStruct((owned2, stencil, 8 * LANES), BF16),
        in_specs=[smem()] + [vmem()] * parts,
        out_specs=vmem(),
        scratch_shapes=[pltpu.VMEM((owned2 * (stencil + 1) + 1, 8, LANES), F32)] * 2,
        compiler_params=params(),
    )(lists, *arrived[::-1])


def chunks_of(parts):
    order = sorted(range(parts), key=lambda d: (-(d >> 1).bit_count(), -(d & 1), -d))
    pairs = [tuple(order[i : i + 2]) for i in range(0, parts, 2)]
    return pairs[:-2] + [pairs[-2] + pairs[-1]]


def local(
    fine_blocks,
    interp,
    fine_cols,
    fine_slot,
    fine_owner,
    fine_place,
    coarse_interp,
    coarse_cols,
    coarse_slot,
    coarse_owner,
    coarse_place,
):
    rows, stencil, width, _ = fine_blocks.shape
    narrow = interp.shape[1] // width
    parts = lax.axis_size("dom")
    region = lax.axis_index("region")
    dom = lax.axis_index("dom")
    owned = rows // 2
    owned2 = owned // 2
    capacity = max(2, rows // 8)
    capacity2 = max(2, owned // 8)
    where = jnp.stack([region, dom]).astype(I32)

    own = halves(interp)
    halo = neighbours(own, "region")

    size2 = coarse_interp.shape[1]
    group = stencil + 1
    inputs = [
        fine_cols.T,
        fine_slot.T,
        fine_owner.T,
        fine_place.reshape(1, rows),
        coarse_slot.T,
        coarse_owner.T,
        coarse_place.reshape(1, owned),
        coarse_interp,
    ]
    info, stacked = pl.pallas_call(
        functools.partial(
            index_kernel, parts=parts, capacity=capacity, capacity2=capacity2, owned=owned, owned2=owned2
        ),
        out_shape=(
            jax.ShapeDtypeStruct((3 * group, LANES), I32),
            jax.ShapeDtypeStruct((owned + 1, size2 // LANES, LANES), BF16),
        ),
        in_specs=[smem()] + [hbm()] * 9,
        out_specs=(vmem(), vmem()),
        scratch_shapes=[pltpu.VMEM((coarse_interp.size // LANES, LANES), F32), pltpu.VMEM((8, LANES), F32)]
        + [pltpu.VMEM(x.shape, x.dtype) for x in inputs]
        + [pltpu.SemaphoreType.DMA((len(inputs),))],
        compiler_params=params(),
    )(where, *[pltpu.with_memory_space_constraint(x, pltpu.HBM) for x in inputs], own)

    table = lax.all_gather(stacked, "dom", axis=0, tiled=True)
    pitch = owned + 1
    targets = table.reshape((parts, pitch, 2 * group, LANES))[:, owned].reshape(parts * 2 * group, LANES).astype(I32)

    tables = neighbours(table, "region")
    arrived = [None] * parts
    chunks = chunks_of(parts)
    sent = ()
    for n, offsets in enumerate(chunks):
        waited = tuple(sent[:1])
        if n == 2:
            waited = waited + tables
        if n >= 3:
            waited = waited + tuple(arrived[d] for d in chunks[n - 3])
        sent = level_one(info, fine_blocks, halo[0], own, halo[1], offsets, capacity, waited)
        for offset, cells in zip(offsets, sent):
            arrived[offset] = exchange(cells, "dom", offset) if offset else cells
    span2 = parts * owned
    inside = coarse_cols % span2
    step2 = table_of(coarse_cols // span2 - region + 1, region)
    index2 = (inside // owned * pitch + inside % owned) * 4 + step2
    picked, turned = pick_rows(index2.T, tables[0], table, tables[1], stacked, sent[0])
    soon = list(chunks[-1][2:]) + [d for offsets in chunks[: (parts // 2) // 2] for d in offsets]
    late = [d for d in range(parts) if d not in soon]
    early, lists = early_sums(
        where,
        targets,
        picked,
        [arrived[d] for d in soon],
        soon,
        late,
        parts,
        capacity,
        capacity2,
        owned,
        stencil,
    )
    outs = owner_level(
        lists,
        picked,
        turned,
        early,
        [arrived[d] for d in late],
        late,
        parts,
        capacity,
        capacity2,
        owned,
        stencil,
    )
    coarse_blocks = outs[0].reshape(stencil, owned, narrow * narrow).transpose(1, 0, 2)
    arrived2 = list(outs[2:])
    for d in range(parts - 1, 0, -1):
        arrived2[d] = exchange(arrived2[d], "dom", d)
    second = final_level(lists, arrived2, parts, capacity2, owned2, stencil)
    return (coarse_blocks, second)


def solution(mesh):
    in_specs = (
        P(("region", "dom"), None, None, None),
        P(("region", "dom"), None),
        P(("region", "dom"), None),
        P(("region", "dom"), None),
        P(("region", "dom"), None),
        P(("region", "dom")),
        P(("region", "dom"), None),
        P(("region", "dom"), None),
        P(("region", "dom"), None),
        P(("region", "dom"), None),
        P(("region", "dom")),
    )
    out_specs = (P(("region", "dom"), None, None), P(("region", "dom"), None, None))
    return jax.shard_map(local, mesh=mesh, in_specs=in_specs, out_specs=out_specs, check_vma=False)
```

```python
import functools

import jax
import jax.numpy as jnp
from jax import lax
from jax.experimental import pallas as pl
from jax.experimental.pallas import tpu as pltpu
from jax.sharding import PartitionSpec as P

BF16 = jnp.bfloat16
F32 = jnp.float32
I32 = jnp.int32
LANES = 128
VMEM_LIMIT = 32 * 1024 * 1024


def vmem():
    return pl.BlockSpec(memory_space=pltpu.VMEM)


def smem():
    return pl.BlockSpec(memory_space=pltpu.SMEM)


def hbm():
    return pl.BlockSpec(memory_space=pl.ANY)


def params():
    return pltpu.CompilerParams(vmem_limit_bytes=VMEM_LIMIT)


def low_lanes(shape, bound):
    return lax.broadcasted_iota(I32, shape, len(shape) - 1) < bound


def exchange(cells, axis, offset):
    count = lax.axis_size(axis)
    return lax.ppermute(cells, axis, [(i, i ^ offset) for i in range(count)])


def partner(index, odd, count):
    other = ((index + odd) ^ 1) - odd
    return other if 0 <= other < count else index


def neighbours(cells, axis):
    count = lax.axis_size(axis)
    return tuple(lax.ppermute(cells, axis, [(i, partner(i, odd, count)) for i in range(count)]) for odd in (1, 0))


def table_of(step, region):
    swapped = jnp.where(region % 2 == 0, step, 2 - step)
    return jnp.where(step == 1, 1, swapped)


def halves_kernel(flat_ref, out_ref, rows_ref, wide_ref, sems):
    steps, group = rows_ref.shape[:2]
    deep = rows_ref.shape[2] // LANES
    half = deep // 2
    left = low_lanes((group, LANES), LANES // 2)

    def copy(g):
        return pltpu.make_async_copy(flat_ref.at[pl.ds(g * group, group)], rows_ref.at[g], sems.at[g])

    for g in range(steps):
        copy(g).start()
    for g in range(steps):
        copy(g).wait()
        for t in range(half):
            upper = rows_ref[g, :, pl.ds(t * LANES, LANES)].astype(F32)
            lower = rows_ref[g, :, pl.ds((t + half) * LANES, LANES)].astype(F32)
            even = jnp.where(left, upper, pltpu.roll(lower, LANES // 2, 1))
            odd = jnp.where(left, pltpu.roll(upper, LANES // 2, 1), lower)
            wide_ref[g, pl.ds(2 * t, group, stride=deep), :] = even
            wide_ref[g, pl.ds(2 * t + 1, group, stride=deep), :] = odd
        for r in range(group):
            out_ref[g * group + r] = wide_ref[g, pl.ds(r * deep, deep), :].astype(BF16)


def halves(flat):
    rows, size = flat.shape
    deep = size // LANES
    group = 16
    steps = rows // group
    return pl.pallas_call(
        halves_kernel,
        out_shape=jax.ShapeDtypeStruct((rows, deep, LANES), BF16),
        in_specs=[pl.BlockSpec(memory_space=pltpu.HBM)],
        out_specs=vmem(),
        scratch_shapes=[
            pltpu.VMEM((steps, group, size), BF16),
            pltpu.VMEM((steps, group * deep, LANES), F32),
            pltpu.SemaphoreType.DMA((steps,)),
        ],
        compiler_params=params(),
    )(pltpu.with_memory_space_constraint(flat, pltpu.HBM))


def quarters_of(coarse_ref, quarters_ref, wide_ref):
    count = coarse_ref.shape[0]
    deep = coarse_ref.shape[1] // LANES
    quarter = LANES // 4
    lane = lax.broadcasted_iota(I32, (count, LANES), 1) // quarter
    for t in range(deep // 4):
        tiles = [coarse_ref[:, pl.ds((h * deep // 4 + t) * LANES, LANES)].astype(F32) for h in range(4)]
        for u in range(4):
            total = None
            for h in range(4):
                shift = (h - u) % 4 * quarter
                piece = pltpu.roll(tiles[h], shift, 1) if shift else tiles[h]
                total = piece if total is None else jnp.where(lane == h, piece, total)
            wide_ref[pl.ds(4 * t + u, count, stride=deep), :] = total
    for r in range(count):
        quarters_ref[r] = wide_ref[pl.ds(r * deep, deep), :].astype(BF16)


def owner_order(owner_ref, wide_ref, capacity):
    count = owner_ref.shape[1]
    square = (LANES, LANES)
    down = lax.broadcasted_iota(I32, square, 0).astype(F32)
    along = lax.broadcasted_iota(I32, square, 1).astype(F32)
    wide_ref[...] = jnp.full(wide_ref.shape, -1.0, F32)
    wide_ref[0:1, 0:count] = owner_ref[...].astype(F32)
    owner = wide_ref[0:1, :]
    across = jnp.broadcast_to(owner, square)
    earlier = jnp.where((across == across.T) & (down < along), 1.0, 0.0)
    rank = jnp.sum(earlier, axis=0, keepdims=True)
    position = jnp.where(owner >= 0.0, owner * capacity + rank, -1.0)
    named = jnp.broadcast_to(position, square).T == along
    hit = jnp.sum(jnp.where(named, 1.0, 0.0), axis=0, keepdims=True)
    row = jnp.sum(jnp.where(named, down, 0.0), axis=0, keepdims=True)
    return (row + (1.0 - hit) * count).astype(I32)


def index_kernel(where_ref, *rest, **sizes):
    inputs = rest[:8]
    info_ref, stacked_ref, wide_ref, narrow_ref = rest[9:13]
    locals_ = rest[13:21]
    sems = rest[21]
    copies = [pltpu.make_async_copy(a, b, sems.at[n]) for n, (a, b) in enumerate(zip(inputs, locals_))]
    for copy in copies:
        copy.start()
    for copy in copies:
        copy.wait()
    fill_tables(where_ref, *locals_, info_ref, stacked_ref, wide_ref, narrow_ref, **sizes)


def fill_tables(
    where_ref,
    cols_ref,
    slot_ref,
    owner_ref,
    place_ref,
    slot2_ref,
    owner2_ref,
    place2_ref,
    coarse_ref,
    info_ref,
    stacked_ref,
    wide_ref,
    narrow_ref,
    *,
    parts,
    capacity,
    capacity2,
    owned,
    owned2,
):
    region = where_ref[0]
    dom = where_ref[1]
    stencil, rows = cols_ref.shape
    rows2 = slot2_ref.shape[1]
    group = stencil + 1
    span = parts * rows
    first = region * span
    quarters_of(coarse_ref, stacked_ref, wide_ref)
    info_ref[0:group, :] = jnp.full((group, LANES), stencil * owned, I32)
    info_ref[group : 2 * group, :] = jnp.full((group, LANES), group * owned2, I32)
    info_ref[2 * group :, :] = jnp.full((group, LANES), dom, I32)
    info_ref[0:stencil, 0:rows] = slot_ref[...] * owned + place_ref[...]
    info_ref[group : group + stencil, 0:rows2] = place2_ref[...] * group + slot2_ref[...]
    cols = cols_ref[...]
    step = jnp.where(cols < first, 0, jnp.where(cols >= first + span, 2, 1))
    begin = ((region + step - 1) * parts + dom) * rows
    info_ref[2 * group : 2 * group + stencil, 0:rows] = (cols - begin) * 4 + table_of(step, region)
    info_ref[stencil : stencil + 1, :] = owner_order(owner_ref, narrow_ref, capacity)
    info_ref[group + stencil : 2 * group, :] = owner_order(owner2_ref, narrow_ref, capacity2)
    stacked_ref[rows2] = info_ref[0 : 2 * group, :].astype(F32).astype(BF16)


def terms_kernel(info_ref, blocks_ref, before_ref, own_ref, after_ref, *rest, offsets, capacity, waited):
    outs = rest[waited : waited + len(offsets)]
    buffer_ref, row_sem = rest[waited + len(offsets) :]
    stencil, width = buffer_ref.shape[1], buffer_ref.shape[2]
    half = width // 2
    narrow = LANES // 2
    flat = narrow * narrow // LANES

    dom = info_ref[3 * (stencil + 1) - 1, 0]

    def source_of(offset, r):
        return jnp.minimum(info_ref[stencil, (dom ^ offset) * capacity + r], own_ref.shape[0] - 1)

    def row_copy(n, source):
        return pltpu.make_async_copy(blocks_ref.at[source], buffer_ref.at[n], row_sem.at[n])

    def fetch(n):
        for r in range(capacity):
            row_copy(n * capacity + r, source_of(offsets[n], r)).start()

    fetch(0)
    left = low_lanes((half, LANES), narrow)
    left_flat = low_lanes((flat, LANES), narrow)
    out_row = lax.broadcasted_iota(I32, (narrow, LANES), 0)
    in_col = lax.broadcasted_iota(I32, (narrow, LANES), 1)
    chosen = jnp.where(out_row < flat, 2 * out_row, 2 * (out_row - flat) + 1)
    pick = jnp.where(in_col == chosen, 1.0, 0.0).astype(BF16)
    zero = jnp.zeros((half, LANES), BF16)

    def neighbour(source, k):
        code = info_ref[2 * (stencil + 1) + k, source]
        row = lax.shift_right_logical(code, 2)
        step = code & 3
        return jnp.where(step == 0, before_ref[row], jnp.where(step == 1, own_ref[row], after_ref[row]))

    def one_row(n, source, out_ref, r):
        mine = own_ref[source]
        column = jnp.concatenate([mine, pltpu.roll(mine, narrow, 1)], axis=0)
        turned = lax.dot_general(
            pick, column, (((1,), (1,)), ((), ())), preferred_element_type=F32
        ).astype(BF16)
        products = []
        for k in range(0, stencil, 2):
            one = neighbour(source, k)
            weights = [jnp.where(left, one, zero), jnp.where(left, pltpu.roll(one, narrow, 1), zero)]
            lhs = buffer_ref[n, k]
            if k + 1 < stencil:
                two = neighbour(source, k + 1)
                weights += [jnp.where(left, zero, pltpu.roll(two, narrow, 1)), jnp.where(left, zero, two)]
                lhs = jnp.concatenate([lhs, buffer_ref[n, k + 1]], axis=1)
            products.append(
                jnp.dot(lhs, jnp.concatenate(weights, axis=0), preferred_element_type=F32).astype(BF16)
            )
        term = jnp.dot(turned, jnp.concatenate(products, axis=1), preferred_element_type=F32)
        for k in range(0, stencil, 2):
            pair = term[:, k // 2 * LANES : (k // 2 + 1) * LANES]
            even = pair[:flat].astype(BF16)
            odd = pair[flat:].astype(BF16)
            base = (r * stencil + k) * flat
            out_ref[pl.ds(base, flat), :] = jnp.where(left_flat, even, pltpu.roll(odd, narrow, 1))
            if k + 1 < stencil:
                out_ref[pl.ds(base + flat, flat), :] = jnp.where(left_flat, pltpu.roll(even, narrow, 1), odd)

    for n, offset in enumerate(offsets):
        sources = [source_of(offset, r) for r in range(capacity)]
        for r, source in enumerate(sources):
            row_copy(n * capacity + r, source).wait()
        if n + 1 < len(offsets):
            fetch(n + 1)
        for r, source in enumerate(sources):
            one_row(n * capacity + r, source, outs[n], r)


def level_one(info, blocks, before, own, after, offsets, capacity, waited):
    rows, stencil, width, _ = blocks.shape
    narrow = LANES // 2
    flat = narrow * narrow // LANES
    shape = jax.ShapeDtypeStruct((capacity * stencil * flat, LANES), BF16)
    count = len(offsets) * capacity
    return pl.pallas_call(
        functools.partial(terms_kernel, offsets=offsets, capacity=capacity, waited=len(waited)),
        out_shape=tuple(shape for _ in offsets),
        in_specs=[smem(), hbm(), vmem(), vmem(), vmem()] + [hbm()] * len(waited),
        out_specs=tuple(vmem() for _ in offsets),
        scratch_shapes=[
            pltpu.VMEM((count, stencil, width, width), BF16),
            pltpu.SemaphoreType.DMA((count,)),
        ],
        compiler_params=params(),
    )(
        info,
        pltpu.with_memory_space_constraint(blocks, pltpu.HBM),
        before,
        own,
        after,
        *waited,
    )


def pick_kernel(index_ref, first_ref, own_ref, second_ref, mine_ref, waited_ref, out_ref, turned_ref):
    stencil, count = index_ref.shape
    quarter = LANES // 4
    narrow = LANES // 2

    def body(q, carry):
        for k in range(stencil):
            code = index_ref[k, q]
            row = lax.shift_right_logical(code, 2)
            step = code & 3
            out_ref[q * stencil + k] = jnp.where(
                step == 0, first_ref[row], jnp.where(step == 1, own_ref[row], second_ref[row])
            )
        return carry

    lax.fori_loop(0, count, body, 0, unroll=4)
    square = (LANES, LANES)
    row = lax.broadcasted_iota(I32, square, 0)
    lane = lax.broadcasted_iota(I32, square, 1)
    old = row // quarter * quarter + row % 8 * 4 + row % quarter // 8
    pick = jnp.where(lane == old, 1.0, 0.0).astype(BF16)
    new = lax.broadcasted_iota(I32, (narrow, narrow), 0)
    old = lax.broadcasted_iota(I32, (narrow, narrow), 1)
    order = jnp.where(old == new % quarter * 2 + new // quarter, 1.0, 0.0).astype(BF16)
    block = lax.broadcasted_iota(I32, (16, LANES), 1) // quarter
    columns = []
    for g in range(count // 4):
        pieces = []
        for h in range(4):
            total = None
            for n in range(4):
                shift = (n - h) % 4 * quarter
                piece = mine_ref[4 * g + n]
                piece = pltpu.roll(piece, shift, 1) if shift else piece
                total = piece if total is None else jnp.where(block == n, piece, total)
            pieces.append(total)
        columns.append(jnp.concatenate(pieces, axis=0))
    ordered = [jnp.dot(order, column, preferred_element_type=F32).astype(BF16) for column in columns]
    for g, column in enumerate(ordered):
        turned = lax.dot_general(pick, column, (((1,), (1,)), ((), ())), preferred_element_type=F32).astype(BF16)
        for n in range(4):
            turned_ref[4 * g + n] = turned[n * quarter : (n + 1) * quarter]


def pick_rows(index, first, own, second, mine, waited):
    stencil, count = index.shape
    return pl.pallas_call(
        pick_kernel,
        out_shape=(
            jax.ShapeDtypeStruct((count * stencil,) + own.shape[1:], own.dtype),
            jax.ShapeDtypeStruct((count, LANES // 4, LANES // 2), own.dtype),
        ),
        in_specs=[smem(), vmem(), vmem(), vmem(), vmem(), hbm()],
        out_specs=(vmem(), vmem()),
        compiler_params=params(),
    )(index, first, own, second, mine, waited)


def add_terms(part_ref, target_of, sum_ref, capacity, stencil):
    flat = sum_ref.shape[1]
    for r in range(capacity):
        for k in range(stencil):
            term = part_ref[pl.ds((r * stencil + k) * flat, flat), :].astype(F32)
            sum_ref[target_of(r, k)] += term


def early_kernel(where_ref, table_ref, *rest, soon, late, parts, capacity, capacity2, owned, stencil):
    sum_ref, lists_ref = rest[-2:]
    dom = where_ref[1]
    group = stencil + 1

    def row_of(d, level, slot):
        return table_ref[((dom ^ d) * 2 + level) * group + stencil, slot]

    def target_at(d, level, row, k):
        return table_ref[((dom ^ d) * 2 + level) * group + k, row]

    at = 0
    for d in range(parts):
        for r in range(capacity2):
            row = table_ref[(dom * 2 + 2) * group - 1, (dom ^ d) * capacity2 + r]
            lists_ref[at] = jnp.minimum(row, owned - 1)
            at += 1
    for d in late:
        for r in range(capacity):
            row = row_of(d, 0, dom * capacity + r)
            for k in range(stencil):
                lists_ref[at] = target_at(d, 0, row, k)
                at += 1
    for d in range(parts):
        for r in range(capacity2):
            row = row_of(d, 1, dom * capacity2 + r)
            for k in range(stencil):
                lists_ref[at] = target_at(d, 1, row, k)
                at += 1
    sum_ref[...] = jnp.zeros(sum_ref.shape, F32)
    for d, part_ref in zip(soon, rest):
        rows = [row_of(d, 0, dom * capacity + r) for r in range(capacity)]
        add_terms(part_ref, lambda r, k: target_at(d, 0, rows[r], k), sum_ref, capacity, stencil)


def early_sums(where, table, waited, arrived, soon, late, parts, capacity, capacity2, owned, stencil):
    sizes = dict(parts=parts, capacity=capacity, capacity2=capacity2, owned=owned, stencil=stencil)
    count = parts * capacity2 * (stencil + 1) + len(late) * capacity * stencil
    return pl.pallas_call(
        functools.partial(early_kernel, soon=soon, late=late, **sizes),
        out_shape=(
            jax.ShapeDtypeStruct((stencil * owned + 1, LANES // 4, LANES), F32),
            jax.ShapeDtypeStruct((count,), I32),
        ),
        in_specs=[smem(), smem()] + [vmem()] * len(soon) + [hbm()],
        out_specs=(vmem(), smem()),
        compiler_params=params(),
    )(where, table, *arrived, waited)


def owner_kernel(
    lists_ref,
    picked_ref,
    own_ref,
    early_ref,
    *rest,
    parts,
    offsets,
    capacity,
    capacity2,
    owned,
    stencil,
):
    arrived = rest[: len(offsets)]
    out_ref = rest[len(offsets)]
    sum_ref = rest[len(offsets) + 1]
    sends = rest[len(offsets) + 2 : len(offsets) + 2 + parts]
    (term_ref,) = rest[len(offsets) + 2 + parts :]
    flat = sum_ref.shape[1]
    narrow = LANES // 2
    for n, part_ref in enumerate(arrived):
        first = parts * capacity2 + n * capacity * stencil
        add_terms(part_ref, lambda r, k: lists_ref[first + r * stencil + k], sum_ref, capacity, stencil)

    left = low_lanes((flat, LANES), narrow)
    quarter = LANES // 4
    eighth = lax.broadcasted_iota(I32, (8, LANES), 1) // quarter
    block = lax.broadcasted_iota(I32, (16, LANES), 1) // quarter
    none = jnp.zeros((16, LANES), BF16)

    batch = 4

    def second(step, carry):
        places = [(step * batch + n, r) for n in range(batch) for r in range(capacity2)]
        names = [lists_ref[d * capacity2 + r] for d, r in places]
        products = []
        for q in names:
            rows = []
            weights = []
            for k in range(0, stencil, 2):
                one = sum_ref[k * owned + q].astype(BF16)
                out_ref[k * owned + q] = one
                if k + 1 < stencil:
                    two = sum_ref[(k + 1) * owned + q].astype(BF16)
                    out_ref[(k + 1) * owned + q] = two
                else:
                    two = jnp.zeros((flat, LANES), BF16)
                even = jnp.where(left, one, pltpu.roll(two, narrow, 1))
                odd = jnp.where(left, pltpu.roll(one, narrow, 1), two)
                rows.append(jnp.concatenate([even, odd], axis=0))
            for k in range(stencil):
                packed = picked_ref[q * stencil + k]
                for h in range(4):
                    shift = (k - h) % 4 * quarter
                    turned = pltpu.roll(packed, shift, 1) if shift else packed
                    weights.append(jnp.where(block == k % 4, turned, none))
            groups = []
            for g in range((stencil + 3) // 4):
                lhs = jnp.concatenate(rows[2 * g : 2 * g + 2], axis=1)
                rhs = jnp.concatenate(weights[16 * g : 16 * g + 16], axis=0)
                product = jnp.dot(lhs[:, : rhs.shape[0]], rhs, preferred_element_type=F32)
                groups.append(product.astype(BF16))
            products.append(jnp.concatenate(groups, axis=1))
        terms = [jnp.dot(own_ref[q], p, preferred_element_type=F32) for q, p in zip(names, products)]
        for (d, r), term in zip(places, terms):
            for k in range(stencil):
                g = k // 4
                total = None
                for w in range(4):
                    piece = term[w * 8 : (w + 1) * 8, g * LANES : (g + 1) * LANES]
                    shift = (w - k) % 4 * quarter
                    if shift:
                        piece = pltpu.roll(piece, shift, 1)
                    total = piece if total is None else jnp.where(eighth == w, piece, total)
                term_ref[d, pl.ds((r * stencil + k) * 8, 8), :] = total
        return carry

    lax.fori_loop(0, parts // batch, second, 0)
    for d in range(parts):
        sends[d][...] = term_ref[d].astype(BF16)


def owner_level(lists, picked, own, early, arrived, offsets, parts, capacity, capacity2, owned, stencil):
    flat = LANES // 4
    send = jax.ShapeDtypeStruct((capacity2 * stencil * 8, LANES), BF16)
    return pl.pallas_call(
        functools.partial(
            owner_kernel,
            parts=parts,
            offsets=offsets,
            capacity=capacity,
            capacity2=capacity2,
            owned=owned,
            stencil=stencil,
        ),
        out_shape=(
            jax.ShapeDtypeStruct((stencil * owned, flat, LANES), BF16),
            jax.ShapeDtypeStruct(early.shape, F32),
        )
        + (send,) * parts,
        in_specs=[smem()] + [vmem()] * (3 + len(offsets)),
        out_specs=(vmem(),) * (2 + parts),
        scratch_shapes=[pltpu.VMEM((parts, capacity2 * stencil * 8, LANES), F32)],
        input_output_aliases={3: 1},
        compiler_params=params(),
    )(lists, picked, own, early, *arrived)


def final_kernel(lists_ref, *rest, parts, capacity2, stencil):
    arrived = rest[:parts][::-1]
    out_ref = rest[parts]
    sum_ref, other_ref = rest[parts + 1 :]
    deep = stencil + 1
    first = lists_ref.shape[0] - parts * capacity2 * stencil
    other_ref[...] = jnp.zeros(other_ref.shape, F32)
    sum_ref[...] = jnp.zeros(sum_ref.shape, F32)
    for d in range(0, parts, 2):
        pairs = [(sum_ref, d), (other_ref, d + 1)]
        values = [arrived[e][...].astype(F32) for _, e in pairs]
        for r in range(capacity2):
            for k in range(stencil):
                at = r * stencil + k
                for (into_ref, e), value in zip(pairs, values):
                    target = lists_ref[first + e * capacity2 * stencil + at]
                    into_ref[target] += value[at * 8 : (at + 1) * 8]
    for u in range(out_ref.shape[0]):
        for t in range(8):
            tile = sum_ref[pl.ds(u * deep, deep), t, :] + other_ref[pl.ds(u * deep, deep), t, :]
            out_ref[u, :, pl.ds(t * LANES, LANES)] = tile[:stencil].astype(BF16)


def final_level(lists, arrived, parts, capacity2, owned2, stencil):
    return pl.pallas_call(
        functools.partial(final_kernel, parts=parts, capacity2=capacity2, stencil=stencil),
        out_shape=jax.ShapeDtypeStruct((owned2, stencil, 8 * LANES), BF16),
        in_specs=[smem()] + [vmem()] * parts,
        out_specs=vmem(),
        scratch_shapes=[pltpu.VMEM((owned2 * (stencil + 1) + 1, 8, LANES), F32)] * 2,
        compiler_params=params(),
    )(lists, *arrived[::-1])


def chunks_of(parts):
    order = sorted(range(parts), key=lambda d: (-(d >> 1).bit_count(), -(d & 1), -d))
    pairs = [tuple(order[i : i + 2]) for i in range(0, parts, 2)]
    return pairs[:-2] + [pairs[-2] + pairs[-1]]


def local(
    fine_blocks,
    interp,
    fine_cols,
    fine_slot,
    fine_owner,
    fine_place,
    coarse_interp,
    coarse_cols,
    coarse_slot,
    coarse_owner,
    coarse_place,
):
    rows, stencil, width, _ = fine_blocks.shape
    narrow = interp.shape[1] // width
    parts = lax.axis_size("dom")
    region = lax.axis_index("region")
    dom = lax.axis_index("dom")
    owned = rows // 2
    owned2 = owned // 2
    capacity = max(2, rows // 8)
    capacity2 = max(2, owned // 8)
    where = jnp.stack([region, dom]).astype(I32)

    own = halves(interp)
    halo = neighbours(own, "region")

    size2 = coarse_interp.shape[1]
    group = stencil + 1
    inputs = [
        fine_cols.T,
        fine_slot.T,
        fine_owner.T,
        fine_place.reshape(1, rows),
        coarse_slot.T,
        coarse_owner.T,
        coarse_place.reshape(1, owned),
        coarse_interp,
    ]
    info, stacked = pl.pallas_call(
        functools.partial(
            index_kernel, parts=parts, capacity=capacity, capacity2=capacity2, owned=owned, owned2=owned2
        ),
        out_shape=(
            jax.ShapeDtypeStruct((3 * group, LANES), I32),
            jax.ShapeDtypeStruct((owned + 1, size2 // LANES, LANES), BF16),
        ),
        in_specs=[smem()] + [hbm()] * 9,
        out_specs=(vmem(), vmem()),
        scratch_shapes=[pltpu.VMEM((coarse_interp.size // LANES, LANES), F32), pltpu.VMEM((8, LANES), F32)]
        + [pltpu.VMEM(x.shape, x.dtype) for x in inputs]
        + [pltpu.SemaphoreType.DMA((len(inputs),))],
        compiler_params=params(),
    )(where, *[pltpu.with_memory_space_constraint(x, pltpu.HBM) for x in inputs], own)

    table = lax.all_gather(stacked, "dom", axis=0, tiled=True)
    pitch = owned + 1
    targets = table.reshape((parts, pitch, 2 * group, LANES))[:, owned].reshape(parts * 2 * group, LANES).astype(I32)

    tables = neighbours(table, "region")
    arrived = [None] * parts
    chunks = chunks_of(parts)
    sent = ()
    for n, offsets in enumerate(chunks):
        waited = tuple(sent[:1])
        if n == 2:
            waited = waited + tables
        if n >= 3:
            waited = waited + tuple(arrived[d] for d in chunks[n - 3])
        sent = level_one(info, fine_blocks, halo[0], own, halo[1], offsets, capacity, waited)
        for offset, cells in zip(offsets, sent):
            arrived[offset] = exchange(cells, "dom", offset) if offset else cells
    span2 = parts * owned
    inside = coarse_cols % span2
    step2 = table_of(coarse_cols // span2 - region + 1, region)
    index2 = (inside // owned * pitch + inside % owned) * 4 + step2
    picked, turned = pick_rows(index2.T, tables[0], table, tables[1], stacked, sent[0])
    soon = list(chunks[-1][2:]) + [d for offsets in chunks[: (parts // 2) // 2] for d in offsets]
    late = [d for d in range(parts) if d not in soon]
    early, lists = early_sums(
        where,
        targets,
        picked,
        [arrived[d] for d in soon],
        soon,
        late,
        parts,
        capacity,
        capacity2,
        owned,
        stencil,
    )
    outs = owner_level(
        lists,
        picked,
        turned,
        early,
        [arrived[d] for d in late],
        late,
        parts,
        capacity,
        capacity2,
        owned,
        stencil,
    )
    coarse_blocks = outs[0].reshape(stencil, owned, narrow * narrow).transpose(1, 0, 2)
    arrived2 = list(outs[2:])
    for d in range(parts - 1, 0, -1):
        arrived2[d] = exchange(arrived2[d], "dom", d)
    second = final_level(lists, arrived2, parts, capacity2, owned2, stencil)
    return (coarse_blocks, second)


def solution(mesh):
    in_specs = (
        P(("region", "dom"), None, None, None),
        P(("region", "dom"), None),
        P(("region", "dom"), None),
        P(("region", "dom"), None),
        P(("region", "dom"), None),
        P(("region", "dom")),
        P(("region", "dom"), None),
        P(("region", "dom"), None),
        P(("region", "dom"), None),
        P(("region", "dom"), None),
        P(("region", "dom")),
    )
    out_specs = (P(("region", "dom"), None, None), P(("region", "dom"), None, None))
    return jax.shard_map(local, mesh=mesh, in_specs=in_specs, out_specs=out_specs, check_vma=False)
```
